128 devices in a mesh: group: 4 (over y_hi, core), fsdp: 32 (over y_lo, x, z).
Axes of the slice: x: 4, y: 4 (y_hi: 2, y_lo: 2; y = y_hi * 2 + y_lo), z: 4, core: 2. Of those that a mesh axis runs over, the one named last changes fastest.
Arguments:
- hidden: bfloat16 [4, 64, 256, 5120], P('group', 'fsdp'), may hold values from -600 to 600
- norm_gain: float32 [5120], replicated, may hold values from 0.1 to 1.9
- queries: bfloat16 [4, 64, 256, 2560], P('group', 'fsdp'), may hold values from -800 to 800
- out_grad: bfloat16 [4, 64, 256, 2560], P('group', 'fsdp'), may hold values from -6 to 6
- kv_inner: bfloat16 [4, 5120, 1024], P('group', 'fsdp'), may hold values from -6 to 6
- kv_outer: float32 [5120, 1024], P('fsdp'), may hold values from -6 to 6
- momentum: float32 [5120, 1024], P('fsdp'), may hold values from -2 to 2
Outputs:
- blended: bfloat16 [4, 5120, 1024], P('group', 'fsdp')
- outer_new: float32 [5120, 1024], P('fsdp')
- momentum_new: float32 [5120, 1024], P('fsdp')
The draws below stay inside these ranges and needn't reach their ends.
All inputs are finite; a program needn't handle non-finite values. Where the reference program divides by a largest or mean magnitude, that divisor is 1e-20 or more.
Results may differ from the reference program's by a relative error of at most 0.025.
The reference program's roundings to bfloat16 on the way (of `rows_in`, `kv_rows`, `kv_grad`, `scales` and `coded`) count: a program that leaves them out, or rounds other values in their place, can miss the bound.
Values may be sent and summed in bfloat16 or wider, within the bound.
A program may use at most 128 MiB of HBM per device.

```python
import math
import jax
import jax.numpy as jnp
from jax import lax

D = 5120
HD = 128
SEQ = 256
QBLOCK = 128
SEQS_DEV = 2
SEQS = 64
QW = 2560
KVC = 1024
N_GROUP = 4


def draw_hidden(key, part):
    first, second = jax.random.split(key)
    third = jax.random.fold_in(key, 3)
    shape = (N_GROUP, SEQS, SEQ, D)
    row_scale = jnp.exp(jax.random.uniform(second, (N_GROUP, SEQS, SEQ, 1), jnp.float32, 0.0, math.log(10.0)))
    col_scale = jnp.exp(jax.random.uniform(third, (D,), jnp.float32, 0.0, math.log(10.0)))
    values = jnp.clip(jax.random.normal(first, shape, jnp.float32), -6.0, 6.0) * (row_scale * col_scale)
    return jnp.clip(values, -600.0, 600.0).astype(jnp.bfloat16)


def draw_queries(key, part):
    first = jax.random.fold_in(key, 0)
    shape = (N_GROUP, SEQS, SEQ, QW)
    base = jnp.clip(jax.random.normal(first, shape, jnp.float32), -6.0, 6.0)
    return jnp.clip(base, -800.0, 800.0).astype(jnp.bfloat16)


def level_of(stream_key, dims, shards, least, largest):
    factor_of = 1.0
    for axis_at, blocks in shards:
        heights = jax.random.uniform(jax.random.fold_in(jax.random.fold_in(stream_key, 6), axis_at), (blocks,), jnp.float32, least / len(shards), largest / len(shards))
        factor_of = factor_of * jnp.repeat(jnp.exp(heights), dims[axis_at] // blocks).reshape((-1,) + (1,) * (len(dims) - 1 - axis_at))
    return factor_of


def gaussian(own_key, shape, width, reach, cuts=(), held_as=jnp.bfloat16):
    drawn = jax.random.normal(own_key, shape, jnp.float32) * width
    if len(cuts) > 0:
        drawn = level_of(own_key, shape, cuts, -0.22, 0.18) * drawn
    return jnp.clip(drawn, min=-reach, max=reach).astype(held_as)


def setup_inputs(seed: int = 0) -> dict:
    key_list = jax.random.split(jax.random.key(seed), 8)
    hidden = draw_hidden(jax.random.fold_in(key_list[7], 71), 0)
    norm_gain = jnp.clip(1.0 + 0.18 * jax.random.normal(key_list[1], (D,), jnp.float32), 0.1, 1.9)
    queries = draw_queries(jax.random.fold_in(key_list[7], 71), 0)
    out_grad = gaussian(key_list[3], (N_GROUP, SEQS, SEQ, QW), 1.0, 6.0, ((0, 4), (1, 32)))
    kv_inner = gaussian(key_list[4], (N_GROUP, D, KVC), 1.0, 6.0, ((0, 4), (1, 32)))
    kv_outer = gaussian(key_list[5], (D, KVC), 1.0, 6.0, ((0, 32),), jnp.float32)
    momentum = gaussian(key_list[6], (D, KVC), 0.3, 2.0, ((0, 32),), jnp.float32)
    return dict(hidden=hidden, norm_gain=norm_gain, queries=queries, out_grad=out_grad, kv_inner=kv_inner, kv_outer=kv_outer, momentum=momentum)


inner_rate = 0.25
outer_rate = 0.7
momentum_decay = 0.9
blend_share = 0.5
norm_eps = 1e-06
scale_eps = 1e-06

def normed_rows(hidden_rows, norm_gain):
    looked = hidden_rows.reshape(-1, hidden_rows.shape[-1]).astype(jnp.float32)
    mean_sq = lax.optimization_barrier(jnp.mean(looked * looked, axis=-1, keepdims=True))
    return (looked * lax.rsqrt(mean_sq + norm_eps) * norm_gain).astype(jnp.bfloat16)

def attend(queries, kv_rows):
    seq_count, length, query_width = queries.shape
    kv_width = kv_rows.shape[-1] // 2
    kv_heads = kv_width // HD
    repeat = query_width // (kv_heads * HD)
    query_h = queries.reshape(seq_count, length, kv_heads, repeat, HD)
    key_h = kv_rows[..., :kv_width].reshape(seq_count, length, kv_heads, HD)
    value_h = kv_rows[..., kv_width:].reshape(seq_count, length, kv_heads, HD)
    scores = jnp.einsum('slgrd,smgd->sgrlm', query_h, key_h, preferred_element_type=jnp.float32) * HD ** (-0.5)
    places = jnp.arange(length)
    causal = places[None, :] <= places[:, None]
    scores = jnp.where(causal, scores, -1e+30)
    highest = lax.stop_gradient(lax.optimization_barrier(jnp.max(scores, axis=-1, keepdims=True)))
    exp_scores = jnp.exp(scores - highest)
    prob_rows = (exp_scores / lax.optimization_barrier(jnp.sum(exp_scores, axis=-1, keepdims=True))).astype(jnp.bfloat16)
    mixed_out = jnp.einsum('sgrlm,smgd->slgrd', prob_rows, value_h, preferred_element_type=jnp.float32)
    return mixed_out.reshape(seq_count, length, query_width)

def kv_grads(queries, kv_rows, out_grad):

    def loss_part(kv_value):
        return attend(queries, kv_value)
    _, pullback = jax.vjp(loss_part, kv_rows)
    return pullback(out_grad.astype(jnp.float32))[0]

def quantize(delta):
    row_count = delta.shape[0]
    shaped = delta.reshape(row_count, -1, QBLOCK)
    scales = (lax.optimization_barrier(jnp.max(jnp.abs(shaped), axis=-1)) + scale_eps).astype(jnp.bfloat16)
    coded = (shaped / scales.astype(jnp.float32)[..., None]).astype(jnp.bfloat16)
    return (coded.reshape(row_count, -1), scales)

def dequantize(coded, scales):
    row_count = coded.shape[0]
    shaped = coded.reshape(row_count, scales.shape[1], -1).astype(jnp.float32)
    return (shaped * scales.astype(jnp.float32)[..., None]).reshape(row_count, -1)

def reference(hidden, norm_gain, queries, out_grad, kv_inner, kv_outer, momentum):
    inv_root = D ** (-0.5)
    groups = kv_inner.shape[0]
    seq_count = hidden.shape[1]
    block_count = seq_count // SEQS_DEV
    fresh_list = []
    totals = jnp.zeros(kv_outer.shape, kv_outer.dtype)
    for group_idx in range(groups):
        rows_in = normed_rows(hidden[group_idx], norm_gain)
        kv_rows = (jnp.dot(rows_in, kv_inner[group_idx], preferred_element_type=jnp.float32) * inv_root).astype(jnp.bfloat16)
        kv_blocks = kv_rows.reshape(block_count, SEQS_DEV, SEQ, kv_rows.shape[-1])
        query_blocks = queries[group_idx].reshape(block_count, SEQS_DEV, SEQ, queries.shape[-1])
        cotan_blocks = out_grad[group_idx].reshape(block_count, SEQS_DEV, SEQ, out_grad.shape[-1])
        kv_grad = lax.map(lambda triple: kv_grads(triple[0], triple[1], triple[2]), (query_blocks, kv_blocks, cotan_blocks))
        grad_blocks = kv_grad.reshape(block_count, SEQS_DEV * SEQ, kv_rows.shape[-1])
        row_blocks = rows_in.reshape(block_count, SEQS_DEV * SEQ, rows_in.shape[-1])

        def add_block(total, pair):
            partial_sum = lax.dot_general(pair[0], pair[1], (((0,), (0,)), ((), ())), preferred_element_type=jnp.float32) * inv_root
            partial_sum = lax.optimization_barrier(partial_sum.astype(jnp.bfloat16))
            return (total + partial_sum.astype(total.dtype), None)
        gradient, _ = lax.scan(add_block, jnp.zeros(kv_outer.shape, kv_outer.dtype), (row_blocks, grad_blocks))
        fresh = kv_inner[group_idx].astype(jnp.float32) - inner_rate * gradient
        fresh_list.append(fresh)
        coded, scales = quantize(kv_outer - fresh)
        totals = totals + dequantize(coded, scales)
    average = totals / groups
    momentum_new = momentum_decay * momentum + average
    outer_new = kv_outer - outer_rate * (momentum_decay * momentum_new + average)
    blended = jnp.stack([(blend_share * fresh + (1.0 - blend_share) * outer_new).astype(jnp.bfloat16) for fresh in fresh_list])
    return (blended, outer_new, momentum_new)
```

```python
import functools
import jax
import jax.numpy as jnp
from jax import lax
from jax.experimental import pallas as pl
from jax.experimental.pallas import tpu as pltpu
from jax.sharding import Mesh
from jax.sharding import PartitionSpec as P

D = 5120
HD = 128
KVC = 1024
TOK = 512
ROWS = 160
QBLOCK = 128
GROUP = ("hi", "core")
FSDP = ("lo", "x", "z")
MESH = pl.DeviceIdType.MESH
BF = jnp.bfloat16
F32 = jnp.float32


inner_rate = 0.25
outer_rate = 0.7
momentum_decay = 0.9
blend_share = 0.5
norm_eps = 1e-06
scale_eps = 1e-06


def piece_cols(p):
    return (p // 2) * 128 + (p % 2) * 512


class Place:
    def __init__(self):
        self.y = lax.axis_index("lo")
        self.x = lax.axis_index("x")
        self.z = lax.axis_index("z")
        self.yo = 1 - self.y

    def names(self, p):
        return ("x", "z") if p % 2 == 0 else ("z", "x")

    def at(self, p, first, off):
        v = getattr(self, self.names(p)[0 if first else 1])
        return lax.rem(v + (off + 4), 4)

    def dev(self, p, first, off):
        return {self.names(p)[0 if first else 1]: self.at(p, first, off)}

    def row(self, ref, p, y, c_off):
        c = self.at(p, False, c_off)
        if p % 2 == 0:
            return ref.at[p, y, :, c]
        return ref.at[p, y, c]

    def block(self, ref, p, y, a_off, c_off):
        a, c = self.at(p, True, a_off), self.at(p, False, c_off)
        if p % 2 == 0:
            return ref.at[p, y, a, c]
        return ref.at[p, y, c, a]


def remote(src, dst, send, recv, dev):
    return pltpu.make_async_remote_copy(
        src_ref=src, dst_ref=dst, send_sem=send, recv_sem=recv, device_id=dev, device_id_type=MESH
    )


def meet(devs):
    barrier = pltpu.get_barrier_semaphore()
    for dev in devs:
        pl.semaphore_signal(barrier, inc=1, device_id=dev, device_id_type=MESH)
    pl.semaphore_wait(barrier, len(devs))


class Gather:
    def __init__(self, place, w8, send, recv):
        self.place, self.w8, self.send, self.recv = place, w8, send, recv

    def copy(self, p, k):
        pc, w = self.place, self.w8
        plus = (p // 2) % 2 == 0
        src, dev = {
            0: lambda: (pc.block(w, p, pc.y, 0, 0), pc.dev(p, True, 1)),
            1: lambda: (pc.block(w, p, pc.y, 0, 0), pc.dev(p, True, -1)),
            2: lambda: (
                pc.block(w, p, pc.y, -1 if plus else 1, 0),
                pc.dev(p, True, 1 if plus else -1),
            ),
            3: lambda: (pc.row(w, p, pc.y, 0), {"lo": pc.yo}),
            4: lambda: (pc.row(w, p, pc.y, 0), pc.dev(p, False, 1)),
            5: lambda: (pc.row(w, p, pc.yo, 0), pc.dev(p, False, 1)),
            6: lambda: (pc.row(w, p, pc.y, 0), pc.dev(p, False, -1)),
            7: lambda: (pc.row(w, p, pc.yo, 0), pc.dev(p, False, -1)),
            8: lambda: (pc.row(w, p, pc.y, -1), pc.dev(p, False, 1)),
            9: lambda: (pc.row(w, p, pc.yo, 1), pc.dev(p, False, -1)),
        }[k]()
        return remote(src, src, self.send.at[p, k], self.recv.at[p, k], dev)

    def start(self, p, k):
        self.copy(p, k).start()

    def landed(self, p, k):
        self.copy(p, k).wait_recv()

    def stage(self, p, s):
        start, landed = functools.partial(self.start, p), functools.partial(self.landed, p)
        if s == 0:
            start(0)
            start(1)
        elif s == 1:
            landed(0)
            landed(1)
            start(2)
        elif s == 2:
            landed(2)
            start(3)
            start(4)
            start(6)
        elif s == 3:
            landed(3)
            start(5)
            start(7)
            landed(4)
            start(8)
        elif s == 4:
            landed(7)
            start(9)
        elif s == 5:
            for k in (5, 6, 8, 9):
                landed(k)

    def drain(self):
        for p in range(8):
            for k in range(10):
                self.copy(p, k).wait_send()


def norm_rows(rows, gain, start, count):
    def step(i, carry):
        at = pl.ds(pl.multiple_of(start + i * 16, 16), 16)
        looked = rows[at, :].astype(F32)
        mean_sq = jnp.mean(looked * looked, axis=-1, keepdims=True)
        looked = rows[at, :].astype(F32)
        rows[at, :] = (looked * lax.rsqrt(mean_sq + norm_eps) * gain[...]).astype(BF)
        return carry

    lax.fori_loop(0, count // 16, step, 0)


def turn_rows(rows, rows_t, start, count):
    def step(j, carry):
        at = pl.multiple_of((start + j) * 128, 128)
        rows_t[pl.ds(at, 128), :] = rows[:, pl.ds(at, 128)].T
        return carry

    lax.fori_loop(0, count, step, 0)


def project(rows, w8, acc, kv, h):
    inv_root = D ** (-0.5)

    def step(i, carry):
        at = pl.multiple_of(i * 1280, 1280)
        y, x = i // 2, 2 * lax.rem(i, 2)
        pair = [w8[2 * h + e, y, pl.ds(x, 2)].reshape(1280, 128) for e in range(2)]
        acc[...] += jnp.dot(
            rows[:, pl.ds(at, 1280)],
            jnp.concatenate(pair, axis=1),
            preferred_element_type=F32,
        )
        return carry

    acc[...] = jnp.zeros_like(acc)
    lax.fori_loop(0, 4, step, 0)
    out = (acc[...] * inv_root).astype(BF)
    kv[:, h * 128 : h * 128 + 128] = out[:, :128]
    kv[:, 512 + h * 128 : 640 + h * 128] = out[:, 128:]


def interleave(comm, work):
    n = len(comm)
    done = 0
    for i, f in enumerate(comm):
        f()
        upto = (i + 1) * len(work) // n
        for g in work[done:upto]:
            g()
        done = upto


def project_kernel(
    hidden, gain, w, kv, rows_t, rows, w8, acc, send, recv, load_sem, own_sem
):
    pc = Place()
    ga = Gather(pc, w8, send, recv)
    loads = []
    for i in range(8):
        at = slice(i * 64, i * 64 + 64)
        loads.append(pltpu.make_async_copy(hidden.at[at], rows.at[at], load_sem.at[i]))
    owns = []
    for p in range(8):
        c = piece_cols(p)
        owns.append(
            pltpu.make_async_copy(
                w.at[:, c : c + 128], pc.block(w8, p, pc.y, 0, 0), own_sem.at[p]
            )
        )
    for cp in owns:
        cp.start()
    for cp in loads:
        cp.start()
    meet(
        [{"lo": pc.yo}]
        + [pc.dev(p, True, o) for p in range(2) for o in (1, -1)]
    )
    for p in range(8):
        owns[p].wait()
        ga.stage(p, 0)

    def norm(i):
        loads[i].wait()
        norm_rows(rows, gain, i * 64, 64)

    def stage(s, h):
        return [functools.partial(ga.stage, 2 * h + e, s) for e in range(2)]

    first = (
        stage(1, 0) + stage(2, 0) + stage(1, 1) + stage(3, 0) + stage(2, 1) + stage(4, 0)
    )
    interleave(first, [functools.partial(norm, i) for i in range(8)])
    turns = [functools.partial(turn_rows, rows, rows_t, i * 5, 5) for i in range(8)]
    interleave(stage(3, 1) + stage(1, 2) + stage(2, 2) + stage(4, 1) + stage(5, 0), turns[:4])
    project(rows, w8, acc, kv, 0)
    interleave(stage(3, 2) + stage(1, 3) + stage(2, 3) + stage(4, 2) + stage(5, 1), turns[4:])
    project(rows, w8, acc, kv, 1)
    interleave(stage(3, 3) + stage(4, 3) + stage(5, 2), [])
    project(rows, w8, acc, kv, 2)
    interleave(stage(5, 3), [])
    project(rows, w8, acc, kv, 3)
    ga.drain()


def gathered_projection(hidden, gain, w):
    return pl.pallas_call(
        project_kernel,
        out_shape=(
            jax.ShapeDtypeStruct((TOK, KVC), BF),
            jax.ShapeDtypeStruct((D, TOK), BF),
        ),
        in_specs=[
            pl.BlockSpec(memory_space=pl.ANY),
            pl.BlockSpec(memory_space=pltpu.VMEM),
            pl.BlockSpec(memory_space=pl.ANY),
        ],
        out_specs=(
            pl.BlockSpec(memory_space=pltpu.VMEM),
            pl.BlockSpec(memory_space=pltpu.VMEM),
        ),
        scratch_shapes=[
            pltpu.VMEM((TOK, D), BF),
            pltpu.VMEM((8, 2, 4, 4, ROWS, 128), BF),
            pltpu.VMEM((TOK, 256), F32),
            pltpu.SemaphoreType.DMA((8, 10)),
            pltpu.SemaphoreType.DMA((8, 10)),
            pltpu.SemaphoreType.DMA((8,)),
            pltpu.SemaphoreType.DMA((8,)),
        ],
        compiler_params=pltpu.CompilerParams(
            collective_id=0, has_side_effects=True, vmem_limit_bytes=48 * 1024 * 1024
        ),
    )(hidden, gain, w)


def reduced_to_own(tiles, axes, turns):
    shape = [lax.axis_size(a) for a in axes]
    tiles = tiles.reshape(*shape, *tiles.shape[1:])
    tiles = tiles.transpose(*turns, *range(len(axes), tiles.ndim))
    tiles = tiles.reshape(-1, *tiles.shape[len(axes) :])
    for k in turns:
        tiles = lax.psum_scatter(tiles, axes[k], scatter_dimension=0, tiled=True)
    return tiles[0]


def in_blocks(value, dim, length):
    shape = value.shape
    tiles = value.reshape(*shape[:dim], length, shape[dim] // length, *shape[dim + 1 :])
    return jnp.moveaxis(tiles, dim, 0)


def scatter_axes(value, axes, turns, dim):
    length = lax.axis_size(axes)
    return reduced_to_own(in_blocks(value, dim, length), axes, turns)


def laid_out(tiles, dim):
    tiles = jnp.moveaxis(tiles, 0, dim)
    shape = tiles.shape
    return tiles.reshape(*shape[:dim], shape[dim] * shape[dim + 1], *shape[dim + 2 :])


def sent_to_all(value, axis):
    copies = jnp.broadcast_to(value, (lax.axis_size(axis), *value.shape))
    return lax.all_to_all(copies, axis, split_axis=0, concat_axis=0, tiled=True)


def gather_directly(value, axis, dim):
    return laid_out(sent_to_all(value, axis), dim)


def side_by_side(arrays, axis, dim, along):
    both = jnp.concatenate(arrays, axis=along)
    out, at, finished = (gather_directly(both, axis, dim), 0, [])
    for a in arrays:
        finished.append(lax.slice_in_dim(out, at, at + a.shape[along], axis=along))
        at += a.shape[along]
    return tuple(finished)


def attend(queries, kv_rows):
    seq_count, length, query_width = queries.shape
    kv_width = kv_rows.shape[-1] // 2
    kv_heads = kv_width // HD
    repeat = query_width // (kv_heads * HD)
    query_h = queries.reshape(seq_count, length, kv_heads, repeat, HD)
    key_h = kv_rows[..., :kv_width].reshape(seq_count, length, kv_heads, HD)
    value_h = kv_rows[..., kv_width:].reshape(seq_count, length, kv_heads, HD)
    scores = jnp.einsum(
        "slgrd,smgd->sgrlm", query_h, key_h, preferred_element_type=jnp.float32
    ) * HD ** (-0.5)
    places = jnp.arange(length)
    causal = places[None, :] <= places[:, None]
    scores = jnp.where(causal, scores, -1e30)
    highest = lax.stop_gradient(jnp.max(scores, axis=-1, keepdims=True))
    exp_scores = jnp.exp(scores - highest)
    prob_rows = (exp_scores / jnp.sum(exp_scores, axis=-1, keepdims=True)).astype(jnp.bfloat16)
    mixed_out = jnp.einsum(
        "sgrlm,smgd->slgrd", prob_rows, value_h, preferred_element_type=jnp.float32
    )
    return mixed_out.reshape(seq_count, length, query_width)


def kv_grads(queries, kv_rows, out_grad):

    def loss_part(kv_value):
        return attend(queries, kv_value)

    _, pullback = jax.vjp(loss_part, kv_rows)
    return pullback(out_grad.astype(jnp.float32))[0]


def quantize(delta):
    row_count = delta.shape[0]
    shaped = delta.reshape(row_count, -1, QBLOCK)
    scales = (jnp.max(jnp.abs(shaped), axis=-1) + scale_eps).astype(jnp.bfloat16)
    coded = (shaped / scales.astype(jnp.float32)[..., None]).astype(jnp.bfloat16)
    return (coded.reshape(row_count, -1), scales)


def dequantize(coded, scales):
    row_count = coded.shape[0]
    shaped = coded.reshape(row_count, scales.shape[1], -1).astype(jnp.float32)
    return (shaped * scales.astype(jnp.float32)[..., None]).reshape(row_count, -1)


def nesterov(outer_rows, moment_rows, average):
    moment_next = momentum_decay * moment_rows + average
    outer_next = outer_rows - outer_rate * (momentum_decay * moment_next + average)
    return (outer_next, moment_next)


def local(hidden, norm_gain, queries, out_grad, kv_inner, kv_outer, momentum):
    inv_root = D ** (-0.5)
    groups = lax.axis_size(GROUP)
    local_weights = kv_inner[0]
    kv_cols = local_weights.shape[1]
    kv_rows, rows_t = gathered_projection(
        hidden[0].reshape(TOK, D), norm_gain.reshape(1, D), local_weights
    )
    seq_local = queries.shape[1]
    kv_rows = kv_rows.reshape(seq_local, queries.shape[2], kv_cols)
    kv_grad = kv_grads(queries[0], kv_rows, out_grad[0]).reshape(-1, kv_cols)
    product = jnp.dot(rows_t, kv_grad, preferred_element_type=F32) * inv_root
    gradient = scatter_axes(product.astype(BF), FSDP, (1, 2, 0), 0).astype(F32)
    fresh = local_weights.astype(jnp.float32) - inner_rate * gradient
    coded, scales = quantize(kv_outer - fresh)
    all_coded, all_scales = side_by_side((coded[None], scales[None]), GROUP, 0, 2)
    totals = jnp.zeros(kv_outer.shape, jnp.float32)
    for member in range(groups):
        totals = totals + dequantize(all_coded[member], all_scales[member])
    average = totals / groups
    outer_new, momentum_new = nesterov(kv_outer, momentum, average)
    blended = (blend_share * fresh + (1.0 - blend_share) * outer_new).astype(jnp.bfloat16)
    return (blended[None], outer_new, momentum_new)


def solution(mesh):
    split = Mesh(
        mesh.devices.reshape(2, 2, 2, 4, 4), GROUP + FSDP
    )
    return jax.shard_map(
        local,
        mesh=split,
        in_specs=(
            P(GROUP, FSDP, None, None),
            P(),
            P(GROUP, FSDP, None, None),
            P(GROUP, FSDP, None, None),
            P(GROUP, FSDP, None),
            P(FSDP, None),
            P(FSDP, None),
        ),
        out_specs=(P(GROUP, FSDP, None), P(FSDP, None), P(FSDP, None)),
        check_vma=False,
    )
```

```python
import functools
import jax
import jax.numpy as jnp
from jax import lax
from jax.experimental import pallas as pl
from jax.experimental.pallas import tpu as pltpu
from jax.sharding import Mesh
from jax.sharding import PartitionSpec as P

D = 5120
HD = 128
KVC = 1024
TOK = 512
ROWS = 160
QBLOCK = 128
GROUP = ("hi", "core")
FSDP = ("lo", "x", "z")
MESH = pl.DeviceIdType.MESH
BF = jnp.bfloat16
F32 = jnp.float32


inner_rate = 0.25
outer_rate = 0.7
momentum_decay = 0.9
blend_share = 0.5
norm_eps = 1e-06
scale_eps = 1e-06


def piece_cols(p):
    return (p // 2) * 128 + (p % 2) * 512


class Place:
    def __init__(self):
        self.y = lax.axis_index("lo")
        self.x = lax.axis_index("x")
        self.z = lax.axis_index("z")
        self.yo = 1 - self.y

    def names(self, p):
        return ("x", "z") if p % 2 == 0 else ("z", "x")

    def at(self, p, first, off):
        v = getattr(self, self.names(p)[0 if first else 1])
        return lax.rem(v + (off + 4), 4)

    def dev(self, p, first, off):
        return {self.names(p)[0 if first else 1]: self.at(p, first, off)}

    def row(self, ref, p, y, c_off):
        c = self.at(p, False, c_off)
        if p % 2 == 0:
            return ref.at[p, y, :, c]
        return ref.at[p, y, c]

    def block(self, ref, p, y, a_off, c_off):
        a, c = self.at(p, True, a_off), self.at(p, False, c_off)
        if p % 2 == 0:
            return ref.at[p, y, a, c]
        return ref.at[p, y, c, a]


def remote(src, dst, send, recv, dev):
    return pltpu.make_async_remote_copy(
        src_ref=src, dst_ref=dst, send_sem=send, recv_sem=recv, device_id=dev, device_id_type=MESH
    )


def meet(devs):
    barrier = pltpu.get_barrier_semaphore()
    for dev in devs:
        pl.semaphore_signal(barrier, inc=1, device_id=dev, device_id_type=MESH)
    pl.semaphore_wait(barrier, len(devs))


class Gather:
    def __init__(self, place, w8, send, recv):
        self.place, self.w8, self.send, self.recv = place, w8, send, recv

    def copy(self, p, k):
        pc, w = self.place, self.w8
        plus = (p // 2) % 2 == 0
        src, dev = {
            0: lambda: (pc.block(w, p, pc.y, 0, 0), pc.dev(p, True, 1)),
            1: lambda: (pc.block(w, p, pc.y, 0, 0), pc.dev(p, True, -1)),
            2: lambda: (
                pc.block(w, p, pc.y, -1 if plus else 1, 0),
                pc.dev(p, True, 1 if plus else -1),
            ),
            3: lambda: (pc.row(w, p, pc.y, 0), {"lo": pc.yo}),
            4: lambda: (pc.row(w, p, pc.y, 0), pc.dev(p, False, 1)),
            5: lambda: (pc.row(w, p, pc.yo, 0), pc.dev(p, False, 1)),
            6: lambda: (pc.row(w, p, pc.y, 0), pc.dev(p, False, -1)),
            7: lambda: (pc.row(w, p, pc.yo, 0), pc.dev(p, False, -1)),
            8: lambda: (pc.row(w, p, pc.y, -1), pc.dev(p, False, 1)),
            9: lambda: (pc.row(w, p, pc.yo, 1), pc.dev(p, False, -1)),
        }[k]()
        return remote(src, src, self.send.at[p, k], self.recv.at[p, k], dev)

    def start(self, p, k):
        self.copy(p, k).start()

    def landed(self, p, k):
        self.copy(p, k).wait_recv()

    def stage(self, p, s):
        start, landed = functools.partial(self.start, p), functools.partial(self.landed, p)
        if s == 0:
            start(0)
            start(1)
        elif s == 1:
            landed(0)
            landed(1)
            start(2)
        elif s == 2:
            landed(2)
            start(3)
            start(4)
            start(6)
        elif s == 3:
            landed(3)
            start(5)
            start(7)
            landed(4)
            start(8)
        elif s == 4:
            landed(7)
            start(9)
        elif s == 5:
            for k in (5, 6, 8, 9):
                landed(k)

    def drain(self):
        for p in range(8):
            for k in range(10):
                self.copy(p, k).wait_send()


def norm_rows(rows, gain, start, count):
    def step(i, carry):
        at = pl.ds(pl.multiple_of(start + i * 16, 16), 16)
        looked = rows[at, :].astype(F32)
        mean_sq = jnp.mean(looked * looked, axis=-1, keepdims=True)
        looked = rows[at, :].astype(F32)
        rows[at, :] = (looked * lax.rsqrt(mean_sq + norm_eps) * gain[...]).astype(BF)
        return carry

    lax.fori_loop(0, count // 16, step, 0)


def turn_rows(rows, rows_t, start, count):
    def step(j, carry):
        at = pl.multiple_of((start + j) * 128, 128)
        rows_t[pl.ds(at, 128), :] = rows[:, pl.ds(at, 128)].T
        return carry

    lax.fori_loop(0, count, step, 0)


def project(rows, w8, acc, kv, h):
    inv_root = D ** (-0.5)

    def step(i, carry):
        at = pl.multiple_of(i * 1280, 1280)
        y, x = i // 2, 2 * lax.rem(i, 2)
        pair = [w8[2 * h + e, y, pl.ds(x, 2)].reshape(1280, 128) for e in range(2)]
        acc[...] += jnp.dot(
            rows[:, pl.ds(at, 1280)],
            jnp.concatenate(pair, axis=1),
            preferred_element_type=F32,
        )
        return carry

    acc[...] = jnp.zeros_like(acc)
    lax.fori_loop(0, 4, step, 0)
    out = (acc[...] * inv_root).astype(BF)
    kv[:, h * 128 : h * 128 + 128] = out[:, :128]
    kv[:, 512 + h * 128 : 640 + h * 128] = out[:, 128:]


def interleave(comm, work):
    n = len(comm)
    done = 0
    for i, f in enumerate(comm):
        f()
        upto = (i + 1) * len(work) // n
        for g in work[done:upto]:
            g()
        done = upto


def project_kernel(
    hidden, gain, w, kv, rows_t, rows, w8, acc, send, recv, load_sem, own_sem
):
    pc = Place()
    ga = Gather(pc, w8, send, recv)
    loads = []
    for i in range(8):
        at = slice(i * 64, i * 64 + 64)
        loads.append(pltpu.make_async_copy(hidden.at[at], rows.at[at], load_sem.at[i]))
    owns = []
    for p in range(8):
        c = piece_cols(p)
        owns.append(
            pltpu.make_async_copy(
                w.at[:, c : c + 128], pc.block(w8, p, pc.y, 0, 0), own_sem.at[p]
            )
        )
    for cp in owns:
        cp.start()
    for cp in loads:
        cp.start()
    meet(
        [{"lo": pc.yo}]
        + [pc.dev(p, True, o) for p in range(2) for o in (1, -1)]
    )
    for p in range(8):
        owns[p].wait()
        ga.stage(p, 0)

    def norm(i):
        loads[i].wait()
        norm_rows(rows, gain, i * 64, 64)

    def stage(s, h):
        return [functools.partial(ga.stage, 2 * h + e, s) for e in range(2)]

    first = (
        stage(1, 0) + stage(2, 0) + stage(1, 1) + stage(3, 0) + stage(2, 1) + stage(4, 0)
    )
    interleave(first, [functools.partial(norm, i) for i in range(8)])
    turns = [functools.partial(turn_rows, rows, rows_t, i * 5, 5) for i in range(8)]
    interleave(stage(3, 1) + stage(1, 2) + stage(2, 2) + stage(4, 1) + stage(5, 0), turns[:4])
    project(rows, w8, acc, kv, 0)
    interleave(stage(3, 2) + stage(1, 3) + stage(2, 3) + stage(4, 2) + stage(5, 1), turns[4:])
    project(rows, w8, acc, kv, 1)
    interleave(stage(3, 3) + stage(4, 3) + stage(5, 2), [])
    project(rows, w8, acc, kv, 2)
    interleave(stage(5, 3), [])
    project(rows, w8, acc, kv, 3)
    ga.drain()


def gathered_projection(hidden, gain, w):
    return pl.pallas_call(
        project_kernel,
        out_shape=(
            jax.ShapeDtypeStruct((TOK, KVC), BF),
            jax.ShapeDtypeStruct((D, TOK), BF),
        ),
        in_specs=[
            pl.BlockSpec(memory_space=pl.ANY),
            pl.BlockSpec(memory_space=pltpu.VMEM),
            pl.BlockSpec(memory_space=pl.ANY),
        ],
        out_specs=(
            pl.BlockSpec(memory_space=pltpu.VMEM),
            pl.BlockSpec(memory_space=pltpu.VMEM),
        ),
        scratch_shapes=[
            pltpu.VMEM((TOK, D), BF),
            pltpu.VMEM((8, 2, 4, 4, ROWS, 128), BF),
            pltpu.VMEM((TOK, 256), F32),
            pltpu.SemaphoreType.DMA((8, 10)),
            pltpu.SemaphoreType.DMA((8, 10)),
            pltpu.SemaphoreType.DMA((8,)),
            pltpu.SemaphoreType.DMA((8,)),
        ],
        compiler_params=pltpu.CompilerParams(
            collective_id=0, has_side_effects=True, vmem_limit_bytes=48 * 1024 * 1024
        ),
    )(hidden, gain, w)


class Scatter:
    def __init__(self, place, g8, via, near, across, last, send, recv):
        self.place, self.g8, self.send, self.recv = place, g8, send, recv
        self.via, self.near, self.across, self.last = via, near, across, last

    def copy(self, p, k):
        pc, g = self.place, self.g8
        plus = (p // 2) % 2 == 0
        src, dst, dev = {
            0: lambda: (pc.row(g, p, pc.y, 2), self.via.at[p, 0], pc.dev(p, False, 1)),
            1: lambda: (pc.row(g, p, pc.yo, 2), self.via.at[p, 1], pc.dev(p, False, -1)),
            2: lambda: (pc.row(g, p, pc.y, 1), self.near.at[p, 0], pc.dev(p, False, 1)),
            3: lambda: (pc.row(g, p, pc.yo, 1), self.near.at[p, 1], pc.dev(p, False, 1)),
            4: lambda: (pc.row(g, p, pc.y, -1), self.near.at[p, 2], pc.dev(p, False, -1)),
            5: lambda: (pc.row(g, p, pc.yo, -1), self.near.at[p, 3], pc.dev(p, False, -1)),
            6: lambda: (pc.row(g, p, pc.yo, 0), self.across.at[p], {"lo": pc.yo}),
            7: lambda: (
                pc.block(g, p, pc.y, 2, 0),
                self.last.at[p, 2],
                pc.dev(p, True, 1 if plus else -1),
            ),
            8: lambda: (pc.block(g, p, pc.y, 1, 0), self.last.at[p, 0], pc.dev(p, True, 1)),
            9: lambda: (pc.block(g, p, pc.y, -1, 0), self.last.at[p, 1], pc.dev(p, True, -1)),
        }[k]()
        return remote(src, dst, self.send.at[p, k], self.recv.at[p, k], dev)

    def start(self, p, k):
        self.copy(p, k).start()

    def landed(self, p, k):
        self.copy(p, k).wait_recv()

    def add(self, dst, *terms):
        total = dst[...].astype(F32)
        for t in terms:
            total = total + t[...].astype(F32)
        dst[...] = total.astype(BF)

    def add_rows(self, dst, *terms):
        for i in range(4):
            self.add(dst.at[i], *[t.at[i] for t in terms])

    def stage(self, p, s):
        pc, g = self.place, self.g8
        start, landed = functools.partial(self.start, p), functools.partial(self.landed, p)
        plus = (p // 2) % 2 == 0
        if s == 0:
            for k in (0, 1, 3, 4):
                start(k)
        elif s == 1:
            landed(0)
            self.add_rows(pc.row(g, p, pc.y, 1), self.via.at[p, 0])
            start(2)
            landed(1)
            self.add_rows(pc.row(g, p, pc.yo, -1), self.via.at[p, 1])
            start(5)
        elif s == 2:
            landed(3)
            landed(5)
            self.add_rows(pc.row(g, p, pc.yo, 0), self.near.at[p, 1], self.near.at[p, 3])
            start(6)
        elif s == 3:
            landed(2)
            landed(4)
            landed(6)
            self.add_rows(
                pc.row(g, p, pc.y, 0), self.near.at[p, 0], self.near.at[p, 2], self.across.at[p]
            )
            start(7)
            start(9 if plus else 8)
        elif s == 4:
            landed(7)
            self.add(pc.block(g, p, pc.y, 1 if plus else -1, 0), self.last.at[p, 2])
            start(8 if plus else 9)

    def total(self, p):
        pc, g = self.place, self.g8
        self.landed(p, 8)
        self.landed(p, 9)
        own = pc.block(g, p, pc.y, 0, 0)[...].astype(F32)
        return own + self.last[p, 0].astype(F32) + self.last[p, 1].astype(F32)

    def drain(self):
        for p in range(8):
            for k in range(10):
                self.copy(p, k).wait_send()


class Outer:
    def __init__(self, w, outer, moment, fresh, coded, scales, mine, send, recv):
        self.hi, self.core = lax.axis_index("hi"), lax.axis_index("core")
        self.w, self.outer, self.moment, self.fresh = w, outer, moment, fresh
        self.coded, self.scales, self.mine = coded, scales, mine
        self.send, self.recv = send, recv

    def slot(self, flip_hi, flip_core):
        hi = 1 - self.hi if flip_hi else self.hi
        core = 1 - self.core if flip_core else self.core
        return hi * 2 + core

    def copy(self, p, k, arriving):
        buf = self.scales if p == 8 else self.coded
        if arriving:
            s = (self.slot(True, False), self.slot(False, True), self.slot(True, True))[k]
        else:
            s = self.slot(k == 2, False)
        ref = buf.at[s] if p == 8 else buf.at[s, p]
        dev = {"hi": 1 - self.hi} if k == 0 else {"core": 1 - self.core}
        return remote(ref, ref, self.send.at[p, k], self.recv.at[p, k], dev)

    def code(self, p, grad):
        c = piece_cols(p)
        cols = slice(c, c + 128)
        fresh = self.w[:, cols].astype(F32) - inner_rate * grad
        self.fresh[:, cols] = fresh
        delta = self.outer[:, cols] - fresh
        scale = (jnp.max(jnp.abs(delta), axis=1, keepdims=True) + scale_eps).astype(BF)
        scale = scale.astype(F32)
        self.coded[self.slot(False, False), p] = (delta / scale).astype(BF)
        lane = lax.broadcasted_iota(jnp.int32, self.mine.shape, 1)
        self.mine[...] = jnp.where(lane == p, scale, self.mine[...])
        self.copy(p, 0, False).start()
        self.copy(p, 1, False).start()

    def send_scales(self):
        self.scales[self.slot(False, False)] = self.mine[...].astype(BF)
        self.copy(8, 0, False).start()
        self.copy(8, 1, False).start()

    def forward(self, p):
        self.copy(p, 0, True).wait_recv()
        self.copy(p, 2, False).start()

    def arrived(self, p):
        self.copy(p, 1, True).wait_recv()
        self.copy(p, 2, True).wait_recv()

    def finish(self, p, blended, outer_new, moment_new):
        c = piece_cols(p)
        cols = slice(c, c + 128)
        total = jnp.zeros((ROWS, 128), F32)
        for g in range(4):
            total = total + self.coded[g, p].astype(F32) * self.scales[g][:, p : p + 1].astype(F32)
        average = total / 4
        moment_next = momentum_decay * self.moment[:, cols] + average
        outer_next = self.outer[:, cols] - outer_rate * (momentum_decay * moment_next + average)
        moment_new[:, cols] = moment_next
        outer_new[:, cols] = outer_next
        blended[:, cols] = (
            blend_share * self.fresh[:, cols] + (1.0 - blend_share) * outer_next
        ).astype(BF)

    def drain(self):
        for p in range(9):
            for k in range(3):
                self.copy(p, k, False).wait_send()


def dot_nt(a, b):
    return lax.dot_general(a, b, (((1,), (1,)), ((), ())), preferred_element_type=F32)


def attend_back(q, og, kv, kvg, prob, cot, h, s):
    tok = slice(s * 256, s * 256 + 256)
    key = kv[tok, h * 128 : h * 128 + 128]
    val = kv[tok, 512 + h * 128 : 640 + h * 128]
    root = HD ** (-0.5)

    def one(r, carry):
        at = pl.multiple_of((h * 5 + r) * 128, 128)
        for b in range(2):
            m = 128 * (b + 1)
            rows = pl.ds(s * 256 + b * 128, 128)
            qb, gb = q[rows, pl.ds(at, 128)], og[rows, pl.ds(at, 128)]
            sc = dot_nt(key[:m], qb) * root
            keys = lax.broadcasted_iota(jnp.int32, (m, 128), 0)
            places = lax.broadcasted_iota(jnp.int32, (m, 128), 1) + b * 128
            sc = jnp.where(keys <= places, sc, -1e30)
            ex = jnp.exp(sc - jnp.max(sc, axis=0, keepdims=True))
            pr = ex * (1.0 / jnp.sum(ex, axis=0, keepdims=True))
            dp = dot_nt(val[:m], gb).astype(BF).astype(F32)
            prod = pr * dp
            ds = prod - pr * jnp.sum(prod, axis=0, keepdims=True)
            to = pl.ds(pl.multiple_of(r * 256 + b * 128, 128), 128)
            prob[:m, to] = pr.astype(BF)
            cot[:m, to] = ds.astype(BF)
        return carry

    lax.fori_loop(0, 5, one, 0, unroll=UNROLL)
    base = h * 640
    rows = slice(s * 256, s * 256 + 256)
    stack = lambda ref: jnp.concatenate(
        [ref[rows, base + r * 128 : base + r * 128 + 128] for r in range(5)], axis=0
    )
    dk = jnp.dot(cot[...], stack(q), preferred_element_type=F32) * root
    dv = jnp.dot(prob[...], stack(og), preferred_element_type=F32)
    kvg[h, tok, :128] = dk.astype(BF)
    kvg[h, tok, 128:] = dv.astype(BF)


UNROLL = 5


def grad_rows(rows_t, kvg, g8, h, first, count):
    inv_root = D ** (-0.5)

    def step(j, carry):
        j = j + first
        at = pl.multiple_of(j * 640, 640)
        out = jnp.dot(rows_t[pl.ds(at, 640), :], kvg[h], preferred_element_type=F32) * inv_root
        out = out.astype(BF)
        y, x = j // 4, lax.rem(j, 4)
        g8[2 * h, y, x] = out[:, :128].reshape(4, ROWS, 128)
        g8[2 * h + 1, y, x] = out[:, 128:].reshape(4, ROWS, 128)
        return carry

    lax.fori_loop(0, count, step, 0)


def sync_kernel(
    q_any, og_any, kv, rows_any, w, outer, moment, blended, outer_new, moment_new,
    q, og, rows_t, kvg, prob, cot, g8, via, near, across, last, fresh, coded, scales, mine,
    send, recv, x_send, x_recv, load_sem,
):
    pc = Place()
    sc = Scatter(pc, g8, via, near, across, last, send, recv)
    ex = Outer(w, outer, moment, fresh, coded, scales, mine, x_send, x_recv)
    loads = [
        pltpu.make_async_copy(a, b, load_sem.at[i])
        for i, (a, b) in enumerate(((q_any, q), (og_any, og), (rows_any, rows_t)))
    ]
    for cp in loads:
        cp.start()
    prob[...] = jnp.zeros_like(prob)
    cot[...] = jnp.zeros_like(cot)
    mine[...] = jnp.zeros_like(mine)
    meet(
        [{"lo": pc.yo}, {"hi": 1 - ex.hi}, {"core": 1 - ex.core}]
        + [pc.dev(p, True, o) for p in range(2) for o in (1, -1)]
    )
    loads[0].wait()
    loads[1].wait()

    def stage(s, h):
        for e in range(2):
            p = 2 * h + e
            if s < 5:
                sc.stage(p, s)
            elif s == 5:
                ex.code(p, sc.total(p))
            else:
                ex.forward(p)

    def attn(h, s):
        attend_back(q, og, kv, kvg, prob, cot, h, s)

    def grads(h):
        grad_rows(rows_t, kvg, g8, h, 0, 8)

    attn(0, 0)
    attn(0, 1)
    loads[2].wait()
    grads(0)
    stage(0, 0)
    attn(1, 0)
    stage(1, 0)
    attn(1, 1)
    grads(1)
    stage(0, 1)
    stage(2, 0)
    attn(2, 0)
    stage(1, 1)
    stage(3, 0)
    attn(2, 1)
    grads(2)
    stage(0, 2)
    stage(4, 0)
    stage(2, 1)
    attn(3, 0)
    stage(1, 2)
    stage(5, 0)
    stage(3, 1)
    attn(3, 1)
    grads(3)
    stage(0, 3)
    stage(6, 0)
    stage(4, 1)
    stage(2, 2)
    stage(1, 3)
    stage(5, 1)
    stage(3, 2)
    stage(6, 1)
    stage(4, 2)
    stage(2, 3)
    stage(5, 2)
    stage(3, 3)
    stage(6, 2)
    stage(4, 3)
    stage(5, 3)
    ex.send_scales()
    stage(6, 3)
    ex.forward(8)
    for p in range(8):
        ex.arrived(p)
    ex.arrived(8)
    for p in range(8):
        ex.finish(p, blended, outer_new, moment_new)
    sc.drain()
    ex.drain()


def synced(q, og, kv, rows_t, w, outer, moment):
    vm, hbm = pl.BlockSpec(memory_space=pltpu.VMEM), pl.BlockSpec(memory_space=pl.ANY)
    return pl.pallas_call(
        sync_kernel,
        out_shape=(
            jax.ShapeDtypeStruct((ROWS, KVC), BF),
            jax.ShapeDtypeStruct((ROWS, KVC), F32),
            jax.ShapeDtypeStruct((ROWS, KVC), F32),
        ),
        in_specs=[hbm, hbm, vm, hbm, vm, vm, vm],
        out_specs=(vm, vm, vm),
        scratch_shapes=[
            pltpu.VMEM((TOK, 2560), BF),
            pltpu.VMEM((TOK, 2560), BF),
            pltpu.VMEM((D, TOK), BF),
            pltpu.VMEM((4, TOK, 256), BF),
            pltpu.VMEM((256, 1280), BF),
            pltpu.VMEM((256, 1280), BF),
            pltpu.VMEM((8, 2, 4, 4, ROWS, 128), BF),
            pltpu.VMEM((8, 2, 4, ROWS, 128), BF),
            pltpu.VMEM((8, 4, 4, ROWS, 128), BF),
            pltpu.VMEM((8, 4, ROWS, 128), BF),
            pltpu.VMEM((8, 3, ROWS, 128), BF),
            pltpu.VMEM((ROWS, KVC), F32),
            pltpu.VMEM((4, 8, ROWS, 128), BF),
            pltpu.VMEM((4, ROWS, 128), BF),
            pltpu.VMEM((ROWS, 128), F32),
            pltpu.SemaphoreType.DMA((8, 10)),
            pltpu.SemaphoreType.DMA((8, 10)),
            pltpu.SemaphoreType.DMA((9, 3)),
            pltpu.SemaphoreType.DMA((9, 3)),
            pltpu.SemaphoreType.DMA((3,)),
        ],
        compiler_params=pltpu.CompilerParams(
            collective_id=1, has_side_effects=True, vmem_limit_bytes=60 * 1024 * 1024
        ),
    )(q, og, kv, rows_t, w, outer, moment)


def local(hidden, norm_gain, queries, out_grad, kv_inner, kv_outer, momentum):
    own = kv_inner[0]
    kv, rows_t = gathered_projection(hidden[0].reshape(TOK, D), norm_gain.reshape(1, D), own)
    blended, outer_new, moment_new = synced(
        queries[0].reshape(TOK, -1), out_grad[0].reshape(TOK, -1), kv, rows_t, own, kv_outer, momentum
    )
    return (blended[None], outer_new, moment_new)


def solution(mesh):
    split = Mesh(
        mesh.devices.reshape(2, 2, 2, 4, 4), GROUP + FSDP
    )
    return jax.shard_map(
        local,
        mesh=split,
        in_specs=(
            P(GROUP, FSDP, None, None),
            P(),
            P(GROUP, FSDP, None, None),
            P(GROUP, FSDP, None, None),
            P(GROUP, FSDP, None),
            P(FSDP, None),
            P(FSDP, None),
        ),
        out_specs=(P(GROUP, FSDP, None), P(FSDP, None), P(FSDP, None)),
        check_vma=False,
    )
```

```python
import functools
import jax
import jax.numpy as jnp
from jax import lax
from jax.experimental import pallas as pl
from jax.experimental.pallas import tpu as pltpu
from jax.sharding import Mesh
from jax.sharding import PartitionSpec as P

D = 5120
HD = 128
KVC = 1024
TOK = 512
ROWS = 160
QBLOCK = 128
GROUP = ("hi", "core")
FSDP = ("lo", "x", "z")
MESH = pl.DeviceIdType.MESH
BF = jnp.bfloat16
F32 = jnp.float32


inner_rate = 0.25
outer_rate = 0.7
momentum_decay = 0.9
blend_share = 0.5
norm_eps = 1e-06
scale_eps = 1e-06


def piece_cols(p):
    return (p // 2) * 128 + (p % 2) * 512


class Place:
    def __init__(self):
        self.y = lax.axis_index("lo")
        self.x = lax.axis_index("x")
        self.z = lax.axis_index("z")
        self.yo = 1 - self.y

    def names(self, p):
        return ("x", "z") if p % 2 == 0 else ("z", "x")

    def at(self, p, first, off):
        v = getattr(self, self.names(p)[0 if first else 1])
        return lax.rem(v + (off + 4), 4)

    def dev(self, p, first, off):
        return {self.names(p)[0 if first else 1]: self.at(p, first, off)}

    def plane(self, q):
        return self.yo if q else self.y

    def half(self, ref, p, q, c_off, h):
        c = self.at(p, False, c_off)
        low = 2 * (self.at(p, True, 0) // 2)
        two = pl.ds(2 - low if h else low, 2)
        if p % 2 == 0:
            return ref.at[p, self.plane(q), two, c]
        return ref.at[p, self.plane(q), c, two]

    def block(self, ref, p, a_off):
        a, c = self.at(p, True, a_off), self.at(p, False, 0)
        if p % 2 == 0:
            return ref.at[p, self.y, a, c]
        return ref.at[p, self.y, c, a]


def remote(src, dst, send, recv, dev):
    return pltpu.make_async_remote_copy(
        src_ref=src, dst_ref=dst, send_sem=send, recv_sem=recv, device_id=dev, device_id_type=MESH
    )


def meet(devs):
    barrier = pltpu.get_barrier_semaphore()
    for dev in devs:
        pl.semaphore_signal(barrier, inc=1, device_id=dev, device_id_type=MESH)
    pl.semaphore_wait(barrier, len(devs))


def up(p):
    return 1 if (p // 2) % 2 == 0 else -1


class Moves:
    def __init__(self, place, send, recv):
        self.place, self.send, self.recv, self.used = place, send, recv, []

    def copy(self, p, k):
        src, dst, dev = self.ends(p, k)
        return remote(src, dst, self.send.at[p, k], self.recv.at[p, k], dev)

    def start(self, p, *keys):
        for k in keys:
            self.copy(p, k).start()
            self.used.append((p, k))

    def landed(self, p, *keys):
        for k in keys:
            self.copy(p, k).wait_recv()

    def drain(self):
        for p, k in self.used:
            self.copy(p, k).wait_send()


class Gather(Moves):
    def __init__(self, place, w8, send, recv):
        super().__init__(place, send, recv)
        self.w8 = w8

    def ends(self, p, k):
        pc, w = self.place, self.w8
        if k < 3:
            src = pc.block(w, p, (0, 0, -up(p))[k])
            return src, src, pc.dev(p, True, (1, -1, up(p))[k])
        if p in LATE_Y:
            if k < 5:
                h = k - 3
                src, dev = pc.half(w, p, 0, 1 if h else -1, h), pc.dev(p, False, -1 if h else 1)
            elif k < 9:
                d, h = (k - 5) // 2, (k - 5) % 2
                src, dev = pc.half(w, p, 0, 0, h), pc.dev(p, False, -1 if d else 1)
            else:
                c, h = (k - 9) // 2, (k - 9) % 2
                src, dev = pc.half(w, p, 0, (0, -1, 1, 2)[c], h), {"lo": pc.yo}
        elif k < 5:
            src, dev = pc.half(w, p, 0, 0, k - 3), {"lo": pc.yo}
        elif k < 13:
            d, q, h = (k - 5) // 4, (k - 5) // 2 % 2, (k - 5) % 2
            src, dev = pc.half(w, p, q, 0, h), pc.dev(p, False, -1 if d else 1)
        else:
            q, h = (k - 13) // 2, (k - 13) % 2
            src, dev = pc.half(w, p, q, 1 if h else -1, h), pc.dev(p, False, -1 if h else 1)
        return src, src, dev

    def act(self, p, s):
        if p in LATE_Y:
            waits, starts = {
                0: ((), (0, 1)),
                1: ((0, 1), (2, 5, 7, 9)),
                2: ((2,), (8, 6, 10)),
                3: ((5,), (3, 11)),
                4: ((8,), (4, 14)),
                5: ((7,), (13,)),
                6: ((6,), (12,)),
                7: ((3,), (15,)),
                8: ((4,), (16,)),
                9: (tuple(range(9, 17)), ()),
            }[s]
        else:
            waits, starts = {
                0: ((), (0, 1)),
                1: ((0, 1), (2, 3, 5, 9)),
                2: ((2,), (4, 10, 6)),
                3: ((3,), (7, 11)),
                4: ((4,), (12, 8)),
                5: ((5,), (13,)),
                6: ((10,), (14,)),
                7: ((7,), (15,)),
                8: ((12,), (16,)),
                9: ((9, 6, 11, 8, 13, 14, 15, 16), ()),
            }[s]
        self.landed(p, *waits)
        self.start(p, *starts)


def norm_rows(rows, gain, start, count):
    def step(i, carry):
        at = pl.ds(pl.multiple_of(start + i * 16, 16), 16)
        looked = rows[at, :].astype(F32)
        mean_sq = jnp.mean(looked * looked, axis=-1, keepdims=True)
        looked = rows[at, :].astype(F32)
        rows[at, :] = (looked * lax.rsqrt(mean_sq + norm_eps) * gain[...]).astype(BF)
        return carry

    lax.fori_loop(0, count // 16, step, 0)


def turn_rows(rows, rows_t, start, count):
    def step(j, carry):
        at = pl.multiple_of((start + j) * 128, 128)
        rows_t[pl.ds(at, 128), :] = rows[:, pl.ds(at, 128)].T
        return carry

    lax.fori_loop(0, count, step, 0)


def project(rows, w8, acc, kv, h):
    inv_root = D ** (-0.5)

    def step(i, carry):
        at = pl.multiple_of(i * 1280, 1280)
        y, x = i // 2, 2 * lax.rem(i, 2)
        pair = [w8[2 * h + e, y, pl.ds(x, 2)].reshape(1280, 128) for e in range(2)]
        acc[...] += jnp.dot(
            rows[:, pl.ds(at, 1280)],
            jnp.concatenate(pair, axis=1),
            preferred_element_type=F32,
        )
        return carry

    acc[...] = jnp.zeros_like(acc)
    lax.fori_loop(0, 4, step, 0)
    out = (acc[...] * inv_root).astype(BF)
    kv[:, h * 128 : h * 128 + 128] = out[:, :128]
    kv[:, 512 + h * 128 : 640 + h * 128] = out[:, 128:]


def interleave(comm, work):
    n = len(comm)
    done = 0
    for i, f in enumerate(comm):
        f()
        upto = (i + 1) * len(work) // n
        for g in work[done:upto]:
            g()
        done = upto


class Scatter(Moves):
    def __init__(self, place, g8, via, near, across, last, send, recv):
        super().__init__(place, send, recv)
        self.g8 = g8
        self.via, self.near, self.across, self.last = via, near, across, last

    def ends(self, p, k):
        pc, g = self.place, self.g8
        if k < 4:
            q, h = k // 2, k % 2
            return pc.half(g, p, q, 2, h), self.via.at[p, k], pc.dev(p, False, -1 if h else 1)
        if k < 12:
            d, q, h = (k - 4) // 4, (k - 4) // 2 % 2, (k - 4) % 2
            off = -1 if d else 1
            return pc.half(g, p, q, off, h), self.near.at[p, k - 4], pc.dev(p, False, off)
        if k < 14:
            return pc.half(g, p, 1, 0, k - 12), self.across.at[p, k - 12], {"lo": pc.yo}
        block = pc.block(g, p, (2, 1, -1)[k - 14])
        return block, self.last.at[p, k - 14], pc.dev(p, True, (up(p), 1, -1)[k - 14])

    def add(self, dst, *terms):
        total = dst[...].astype(F32)
        for t in terms:
            total = total + t[...].astype(F32)
        dst[...] = total.astype(BF)

    def add_half(self, dst, *terms):
        for i in range(2):
            self.add(dst.at[i], *[t.at[i] for t in terms])

    def act(self, p, s):
        pc, g, via, near = self.place, self.g8, self.via, self.near
        if s == 0:
            self.start(p, 3, 2, 7, 10)
        elif s == 1:
            self.start(p, 1, 0, 5, 8)
        elif s in (2, 3, 6, 7):
            q, h = (1 if s < 4 else 0), 1 - s % 2
            self.landed(p, 2 * q + h)
            self.add_half(pc.half(g, p, q, -1 if h else 1, h), via.at[p, 2 * q + h])
            self.start(p, 4 + h * 4 + q * 2 + h)
        elif s in (4, 5):
            h = 5 - s
            self.landed(p, 6 + h, 10 + h)
            self.add_half(pc.half(g, p, 1, 0, h), near.at[p, 2 + h], near.at[p, 6 + h])
            self.start(p, 12 + h)
        elif s in (8, 9):
            h = 9 - s
            self.landed(p, 4 + h, 8 + h, 12 + h)
            self.add_half(
                pc.half(g, p, 0, 0, h), near.at[p, h], near.at[p, 4 + h], self.across.at[p, h]
            )
            self.start(p, 14 if s == 8 else (16 if up(p) > 0 else 15))
        elif s == 10:
            self.landed(p, 14)
            self.add(pc.block(g, p, up(p)), self.last.at[p, 0])
            self.start(p, 15 if up(p) > 0 else 16)

    def total(self, p):
        self.landed(p, 15, 16)
        own = self.place.block(self.g8, p, 0)[...].astype(F32)
        return own + self.last[p, 1].astype(F32) + self.last[p, 2].astype(F32)


class Outer:
    def __init__(self, w, outer, fresh, coded, scales, mine, send, recv):
        self.hi, self.core = lax.axis_index("hi"), lax.axis_index("core")
        self.w, self.outer, self.fresh = w, outer, fresh
        self.coded, self.scales, self.mine = coded, scales, mine
        self.send, self.recv = send, recv

    def slot(self, flip_hi, flip_core):
        hi = 1 - self.hi if flip_hi else self.hi
        core = 1 - self.core if flip_core else self.core
        return hi * 2 + core

    def copy(self, p, k, arriving):
        buf = self.scales if p == 8 else self.coded
        if arriving:
            s = (self.slot(True, False), self.slot(False, True), self.slot(True, True))[k]
        else:
            s = self.slot(k == 2, False)
        ref = buf.at[s] if p == 8 else buf.at[s, p]
        dev = {"hi": 1 - self.hi} if k == 0 else {"core": 1 - self.core}
        return remote(ref, ref, self.send.at[p, k], self.recv.at[p, k], dev)

    def code(self, p, grad):
        c = piece_cols(p)
        cols = slice(c, c + 128)
        fresh = self.w[:, cols].astype(F32) - inner_rate * grad
        self.fresh[:, cols] = fresh
        delta = self.outer[:, cols] - fresh
        scale = (jnp.max(jnp.abs(delta), axis=1, keepdims=True) + scale_eps).astype(BF)
        scale = scale.astype(F32)
        self.coded[self.slot(False, False), p] = (delta / scale).astype(BF)
        lane = lax.broadcasted_iota(jnp.int32, self.mine.shape, 1)
        self.mine[...] = jnp.where(lane == p, scale, self.mine[...])
        self.copy(p, 0, False).start()
        self.copy(p, 1, False).start()

    def send_scales(self):
        self.scales[self.slot(False, False)] = self.mine[...].astype(BF)
        self.copy(8, 0, False).start()
        self.copy(8, 1, False).start()

    def forward(self, p):
        self.copy(p, 0, True).wait_recv()
        self.copy(p, 2, False).start()

    def arrived(self, p):
        self.copy(p, 1, True).wait_recv()
        self.copy(p, 2, True).wait_recv()

    def finish(self, p, average):
        c = piece_cols(p)
        total = jnp.zeros((ROWS, 128), F32)
        for g in range(4):
            total = total + self.coded[g, p].astype(F32) * self.scales[g][:, p : p + 1].astype(F32)
        average[:, c : c + 128] = total / 4

    def drain(self):
        for p in range(9):
            for k in range(3):
                self.copy(p, k, False).wait_send()


def dot_nt(a, b):
    return lax.dot_general(a, b, (((1,), (1,)), ((), ())), preferred_element_type=F32)


def attend_back(q, og, kv, kvg, prob, cot, h, s):
    tok = slice(s * 256, s * 256 + 256)
    key = kv[tok, h * 128 : h * 128 + 128]
    val = kv[tok, 512 + h * 128 : 640 + h * 128]
    root = HD ** (-0.5)

    def one(r, carry):
        at = pl.multiple_of((h * 5 + r) * 128, 128)
        for b in range(2):
            m = 128 * (b + 1)
            rows = pl.ds(s * 256 + b * 128, 128)
            qb, gb = q[rows, pl.ds(at, 128)], og[rows, pl.ds(at, 128)]
            sc = dot_nt(key[:m], qb) * root
            keys = lax.broadcasted_iota(jnp.int32, (m, 128), 0)
            places = lax.broadcasted_iota(jnp.int32, (m, 128), 1) + b * 128
            sc = jnp.where(keys <= places, sc, -1e30)
            ex = jnp.exp(sc - jnp.max(sc, axis=0, keepdims=True))
            pr = ex * (1.0 / jnp.sum(ex, axis=0, keepdims=True))
            dp = dot_nt(val[:m], gb).astype(BF).astype(F32)
            prod = pr * dp
            ds = prod - pr * jnp.sum(prod, axis=0, keepdims=True)
            to = pl.ds(pl.multiple_of(r * 256 + b * 128, 128), 128)
            prob[:m, to] = pr.astype(BF)
            cot[:m, to] = ds.astype(BF)
        return carry

    lax.fori_loop(0, 5, one, 0, unroll=UNROLL)
    base = h * 640
    rows = slice(s * 256, s * 256 + 256)
    stack = lambda ref: jnp.concatenate(
        [ref[rows, base + r * 128 : base + r * 128 + 128] for r in range(5)], axis=0
    )
    dk = jnp.dot(cot[...], stack(q), preferred_element_type=F32) * root
    dv = jnp.dot(prob[...], stack(og), preferred_element_type=F32)
    kvg[h, tok, :128] = dk.astype(BF)
    kvg[h, tok, 128:] = dv.astype(BF)


UNROLL = 5


def grad_rows(rows_t, kvg, g8, h, y):
    inv_root = D ** (-0.5)

    def one(x, carry):
        at = pl.multiple_of((y * 4 + x) * 640, 640)
        out = jnp.dot(rows_t[pl.ds(at, 640), :], kvg[h], preferred_element_type=F32) * inv_root
        out = out.astype(BF)
        g8[2 * h, y, x] = out[:, :128].reshape(4, ROWS, 128)
        g8[2 * h + 1, y, x] = out[:, 128:].reshape(4, ROWS, 128)
        return carry

    lax.fori_loop(0, 4, one, 0)


def step_kernel(
    hidden, gain_any, w_any, q_any, og_any, outer_any,
    fresh, average,
    gain, w, outer, q, og, rows, rows_t, w8, acc, kv, kvg, prob, cot,
    g8, via, near, across, last, coded, scales, mine,
    ag_send, ag_recv, send, recv, x_send, x_recv, load_sem, own_sem, arg_sem,
):
    pc = Place()
    ga = Gather(pc, w8, ag_send, ag_recv)
    sc = Scatter(pc, g8, via, near, across, last, send, recv)
    ex = Outer(w, outer, fresh, coded, scales, mine, x_send, x_recv)
    owns = []
    for p in range(8):
        c = piece_cols(p)
        owns.append(
            pltpu.make_async_copy(
                w_any.at[:, c : c + 128], pc.block(w8, p, 0), own_sem.at[p]
            )
        )
    loads = []
    for i in range(8):
        at = slice(i * 64, i * 64 + 64)
        loads.append(pltpu.make_async_copy(hidden.at[at], rows.at[at], load_sem.at[i]))
    args = [
        pltpu.make_async_copy(a, b, arg_sem.at[i])
        for i, (a, b) in enumerate(
            (
                (gain_any, gain),
                (q_any, q),
                (og_any, og),
                (w_any, w),
                (outer_any, outer),
            )
        )
    ]
    for cp in owns + args[:1] + loads + args[1:]:
        cp.start()
    meet(
        [{"lo": pc.yo}, {"hi": 1 - ex.hi}, {"core": 1 - ex.core}]
        + [pc.dev(p, True, o) for p in range(2) for o in (1, -1)]
    )
    for p in range(8):
        owns[p].wait()
    args[0].wait()

    def norm(i):
        loads[i].wait()
        norm_rows(rows, gain, i * 64, 64)

    def turn(i):
        turn_rows(rows, rows_t, i * 5, 5)

    def scatter(p, s):
        if s < 11:
            sc.act(p, s)
        elif s == 11:
            ex.code(p, sc.total(p))
        else:
            ex.forward(p)

    def attn(h, s):
        attend_back(q, og, kv, kvg, prob, cot, h, s)

    def grads(h, near):
        grad_rows(rows_t, kvg, g8, h, pc.plane(1 - near))

    def proj(h):
        project(rows, w8, acc, kv, h)

    def clear():
        prob[...] = jnp.zeros_like(prob)
        cot[...] = jnp.zeros_like(cot)
        mine[...] = jnp.zeros_like(mine)
        for cp in args[1:]:
            cp.wait()

    acts = dict(G=ga.act, T=scatter, A=attn, M=grads, P=proj, N=norm, U=turn, C=clear)
    for kind, *nums in ORDER:
        acts[kind](*nums)
    ex.send_scales()
    ex.forward(8)
    for p in range(8):
        ex.arrived(p)
    ex.arrived(8)
    for p in range(8):
        ex.finish(p, average)
    ga.drain()
    sc.drain()
    ex.drain()


LATE_Y = (4, 5)

ORDER = (
    ("G", 0, 0), ("G", 1, 0), ("G", 2, 0), ("G", 3, 0), ("G", 4, 0), ("G", 5, 0), ("G", 6, 0),
    ("G", 7, 0), ("N", 0), ("N", 1), ("N", 2), ("G", 0, 1), ("G", 1, 1), ("G", 2, 1), ("G", 3, 1),
    ("N", 3), ("N", 4), ("G", 0, 2), ("N", 5), ("G", 0, 5), ("G", 0, 3), ("N", 6), ("G", 1, 5),
    ("G", 1, 2), ("N", 7), ("G", 1, 3), ("G", 2, 5), ("G", 3, 5), ("U", 0), ("G", 2, 2), ("U", 1),
    ("U", 2), ("G", 0, 6), ("G", 3, 2), ("U", 3), ("G", 1, 6), ("G", 2, 3), ("U", 4), ("G", 3, 3),
    ("U", 5), ("U", 6), ("G", 0, 4), ("G", 7, 1), ("U", 7), ("C",), ("G", 2, 6), ("G", 3, 6),
    ("G", 0, 7), ("G", 1, 7), ("G", 6, 1), ("G", 1, 4), ("G", 2, 4), ("G", 3, 4), ("G", 0, 8),
    ("G", 2, 7), ("G", 3, 7), ("G", 6, 3), ("G", 7, 5), ("G", 6, 2), ("G", 7, 3), ("G", 1, 8),
    ("G", 6, 5), ("G", 2, 8), ("G", 7, 2), ("G", 3, 8), ("G", 6, 4), ("G", 0, 9), ("G", 4, 1),
    ("G", 7, 4), ("G", 1, 9), ("P", 0), ("G", 5, 1), ("G", 6, 7), ("G", 6, 6), ("G", 7, 7),
    ("G", 7, 6), ("A", 0, 0), ("G", 2, 9), ("G", 3, 9), ("A", 0, 1), ("G", 4, 2), ("G", 6, 8),
    ("G", 7, 8), ("M", 0, 0), ("G", 4, 5), ("G", 5, 5), ("T", 0, 0), ("T", 1, 0), ("M", 0, 1),
    ("G", 4, 3), ("G", 5, 3), ("P", 1), ("G", 4, 4), ("G", 5, 2), ("T", 0, 1), ("T", 1, 1),
    ("G", 6, 9), ("G", 7, 9), ("A", 1, 0), ("G", 4, 6), ("T", 1, 2), ("A", 1, 1), ("T", 0, 3),
    ("T", 1, 3), ("T", 0, 2), ("M", 1, 0), ("G", 5, 7), ("G", 5, 4), ("T", 2, 0), ("T", 3, 0),
    ("M", 1, 1), ("G", 4, 8), ("P", 3), ("T", 0, 7), ("T", 1, 7), ("G", 4, 7), ("T", 0, 6),
    ("T", 1, 6), ("G", 5, 6), ("T", 2, 1), ("T", 3, 1), ("A", 3, 0), ("A", 3, 1), ("G", 5, 8),
    ("T", 2, 3), ("T", 2, 2), ("T", 3, 3), ("T", 3, 2), ("T", 0, 5), ("M", 3, 0), ("T", 1, 5),
    ("T", 6, 0), ("T", 7, 0), ("M", 3, 1), ("G", 4, 9), ("T", 0, 4), ("T", 2, 7), ("T", 2, 6),
    ("T", 3, 7), ("T", 3, 6), ("T", 1, 4), ("T", 6, 1), ("G", 5, 9), ("P", 2), ("T", 2, 5),
    ("T", 3, 5), ("T", 7, 1), ("A", 2, 0), ("T", 2, 4), ("T", 6, 3), ("T", 7, 3), ("T", 6, 2),
    ("T", 7, 2), ("A", 2, 1), ("T", 0, 8), ("T", 0, 9), ("T", 1, 8), ("T", 1, 9), ("T", 3, 4),
    ("T", 6, 7), ("T", 6, 6), ("T", 7, 7), ("T", 7, 6), ("M", 2, 0), ("T", 4, 0), ("T", 5, 0),
    ("M", 2, 1), ("T", 4, 1), ("T", 2, 8), ("T", 2, 9), ("T", 0, 10), ("T", 6, 5), ("T", 7, 5),
    ("T", 5, 1), ("T", 6, 4), ("T", 7, 4), ("T", 1, 10), ("T", 3, 8), ("T", 3, 9), ("T", 4, 2),
    ("T", 5, 2), ("T", 4, 3), ("T", 5, 3), ("T", 2, 10), ("T", 4, 7), ("T", 4, 6), ("T", 0, 11),
    ("T", 6, 8), ("T", 6, 9), ("T", 5, 6), ("T", 5, 7), ("T", 7, 8), ("T", 1, 11), ("T", 3, 10),
    ("T", 7, 9), ("T", 0, 12), ("T", 4, 4), ("T", 5, 4), ("T", 4, 5), ("T", 5, 5), ("T", 2, 11),
    ("T", 1, 12), ("T", 6, 10), ("T", 7, 10), ("T", 3, 11), ("T", 4, 8), ("T", 6, 11),
    ("T", 2, 12), ("T", 5, 8), ("T", 7, 11), ("T", 4, 9), ("T", 3, 12), ("T", 4, 10), ("T", 6, 12),
    ("T", 5, 9), ("T", 5, 10), ("T", 7, 12), ("T", 4, 11), ("T", 5, 11), ("T", 4, 12),
    ("T", 5, 12),
)


def step(*arrays):
    hbm, vm = pl.BlockSpec(memory_space=pl.ANY), pl.BlockSpec(memory_space=pltpu.VMEM)
    return pl.pallas_call(
        step_kernel,
        out_shape=(
            jax.ShapeDtypeStruct((ROWS, KVC), F32),
            jax.ShapeDtypeStruct((ROWS, KVC), F32),
        ),
        in_specs=[hbm] * 6,
        out_specs=(vm, vm),
        scratch_shapes=[
            pltpu.VMEM((1, D), F32),
            pltpu.VMEM((ROWS, KVC), BF),
            pltpu.VMEM((ROWS, KVC), F32),
            pltpu.VMEM((TOK, 2560), BF),
            pltpu.VMEM((TOK, 2560), BF),
            pltpu.VMEM((TOK, D), BF),
            pltpu.VMEM((D, TOK), BF),
            pltpu.VMEM((8, 2, 4, 4, ROWS, 128), BF),
            pltpu.VMEM((TOK, 256), F32),
            pltpu.VMEM((TOK, KVC), BF),
            pltpu.VMEM((4, TOK, 256), BF),
            pltpu.VMEM((256, 1280), BF),
            pltpu.VMEM((256, 1280), BF),
            pltpu.VMEM((8, 2, 4, 4, ROWS, 128), BF),
            pltpu.VMEM((8, 4, 2, ROWS, 128), BF),
            pltpu.VMEM((8, 8, 2, ROWS, 128), BF),
            pltpu.VMEM((8, 2, 2, ROWS, 128), BF),
            pltpu.VMEM((8, 3, ROWS, 128), BF),
            pltpu.VMEM((4, 8, ROWS, 128), BF),
            pltpu.VMEM((4, ROWS, 128), BF),
            pltpu.VMEM((ROWS, 128), F32),
            pltpu.SemaphoreType.DMA((8, 17)),
            pltpu.SemaphoreType.DMA((8, 17)),
            pltpu.SemaphoreType.DMA((8, 17)),
            pltpu.SemaphoreType.DMA((8, 17)),
            pltpu.SemaphoreType.DMA((9, 3)),
            pltpu.SemaphoreType.DMA((9, 3)),
            pltpu.SemaphoreType.DMA((8,)),
            pltpu.SemaphoreType.DMA((8,)),
            pltpu.SemaphoreType.DMA((5,)),
        ],
        compiler_params=pltpu.CompilerParams(
            collective_id=0, has_side_effects=True, vmem_limit_bytes=67043328
        ),
    )(*arrays)


def local(hidden, norm_gain, queries, out_grad, kv_inner, kv_outer, momentum):
    fresh, average = step(
        hidden[0].reshape(TOK, D),
        norm_gain.reshape(1, D),
        kv_inner[0],
        queries[0].reshape(TOK, -1),
        out_grad[0].reshape(TOK, -1),
        kv_outer,
    )
    moment_new = momentum_decay * momentum + average
    outer_new = kv_outer - outer_rate * (momentum_decay * moment_new + average)
    blended = (blend_share * fresh + (1.0 - blend_share) * outer_new).astype(BF)
    return (blended[None], outer_new, moment_new)


def solution(mesh):
    split = Mesh(
        mesh.devices.reshape(2, 2, 2, 4, 4), GROUP + FSDP
    )
    return jax.shard_map(
        local,
        mesh=split,
        in_specs=(
            P(GROUP, FSDP, None, None),
            P(),
            P(GROUP, FSDP, None, None),
            P(GROUP, FSDP, None, None),
            P(GROUP, FSDP, None),
            P(FSDP, None),
            P(FSDP, None),
        ),
        out_specs=(P(GROUP, FSDP, None), P(FSDP, None), P(FSDP, None)),
        check_vma=False,
    )
```

```python
import functools
import jax
import jax.numpy as jnp
from jax import lax
from jax.experimental import pallas as pl
from jax.experimental.pallas import tpu as pltpu
from jax.sharding import Mesh
from jax.sharding import PartitionSpec as P

D = 5120
HD = 128
KVC = 1024
TOK = 512
ROWS = 160
QBLOCK = 128
GROUP = ("hi", "core")
FSDP = ("lo", "x", "z")
MESH = pl.DeviceIdType.MESH
BF = jnp.bfloat16
F32 = jnp.float32


inner_rate = 0.25
outer_rate = 0.7
momentum_decay = 0.9
blend_share = 0.5
norm_eps = 1e-06
scale_eps = 1e-06


def piece_cols(p):
    return (p // 2) * 128 + (p % 2) * 512


class Place:
    def __init__(self):
        self.y = lax.axis_index("lo")
        self.x = lax.axis_index("x")
        self.z = lax.axis_index("z")
        self.yo = 1 - self.y

    def names(self, p):
        return ("x", "z") if p % 2 == 0 else ("z", "x")

    def at(self, p, first, off):
        v = getattr(self, self.names(p)[0 if first else 1])
        return lax.rem(v + (off + 4), 4)

    def dev(self, p, first, off):
        return {self.names(p)[0 if first else 1]: self.at(p, first, off)}

    def plane(self, q):
        return self.yo if q else self.y

    def half(self, ref, p, q, c_off, h):
        c = self.at(p, False, c_off)
        low = 2 * (self.at(p, True, 0) // 2)
        two = pl.ds(2 - low if h else low, 2)
        if p % 2 == 0:
            return ref.at[p, self.plane(q), two, c]
        return ref.at[p, self.plane(q), c, two]

    def block(self, ref, p, a_off):
        a, c = self.at(p, True, a_off), self.at(p, False, 0)
        if p % 2 == 0:
            return ref.at[p, self.y, a, c]
        return ref.at[p, self.y, c, a]


def remote(src, dst, send, recv, dev):
    return pltpu.make_async_remote_copy(
        src_ref=src, dst_ref=dst, send_sem=send, recv_sem=recv, device_id=dev, device_id_type=MESH
    )


def meet(devs):
    barrier = pltpu.get_barrier_semaphore()
    for dev in devs:
        pl.semaphore_signal(barrier, inc=1, device_id=dev, device_id_type=MESH)
    pl.semaphore_wait(barrier, len(devs))


def up(p):
    return 1 if (p // 2) % 2 == 0 else -1


class Moves:
    def __init__(self, place, send, recv):
        self.place, self.send, self.recv, self.used = place, send, recv, []

    def copy(self, p, k):
        src, dst, dev = self.ends(p, k)
        return remote(src, dst, self.send.at[p, k], self.recv.at[p, k], dev)

    def start(self, p, *keys):
        for k in keys:
            self.copy(p, k).start()
            self.used.append((p, k))

    def landed(self, p, *keys):
        for k in keys:
            self.copy(p, k).wait_recv()

    def drain(self):
        for p, k in self.used:
            self.copy(p, k).wait_send()


class Gather(Moves):
    def __init__(self, place, w8, send, recv):
        super().__init__(place, send, recv)
        self.w8 = w8

    def ends(self, p, k):
        pc, w = self.place, self.w8
        if k < 3:
            src = pc.block(w, p, (0, 0, -up(p))[k])
            return src, src, pc.dev(p, True, (1, -1, up(p))[k])
        if p in LATE_Y:
            if k < 5:
                h = k - 3
                src, dev = pc.half(w, p, 0, 1 if h else -1, h), pc.dev(p, False, -1 if h else 1)
            elif k < 9:
                d, h = (k - 5) // 2, (k - 5) % 2
                src, dev = pc.half(w, p, 0, 0, h), pc.dev(p, False, -1 if d else 1)
            else:
                c, h = (k - 9) // 2, (k - 9) % 2
                src, dev = pc.half(w, p, 0, (0, -1, 1, 2)[c], h), {"lo": pc.yo}
        elif k < 5:
            src, dev = pc.half(w, p, 0, 0, k - 3), {"lo": pc.yo}
        elif k < 13:
            d, q, h = (k - 5) // 4, (k - 5) // 2 % 2, (k - 5) % 2
            src, dev = pc.half(w, p, q, 0, h), pc.dev(p, False, -1 if d else 1)
        else:
            q, h = (k - 13) // 2, (k - 13) % 2
            src, dev = pc.half(w, p, q, 1 if h else -1, h), pc.dev(p, False, -1 if h else 1)
        return src, src, dev

    def act(self, p, s):
        if p in LATE_Y:
            waits, starts = {
                0: ((), (0, 1)),
                1: ((0, 1), (2, 5, 7, 9)),
                2: ((2,), (8, 6, 10)),
                3: ((5,), (3, 11)),
                4: ((8,), (4, 14)),
                5: ((7,), (13,)),
                6: ((6,), (12,)),
                7: ((3,), (15,)),
                8: ((4,), (16,)),
                9: (tuple(range(9, 17)), ()),
            }[s]
        else:
            waits, starts = {
                0: ((), (0, 1)),
                1: ((0, 1), (2, 3, 5, 9)),
                2: ((2,), (4, 10, 6)),
                3: ((3,), (7, 11)),
                4: ((4,), (12, 8)),
                5: ((5,), (13,)),
                6: ((10,), (14,)),
                7: ((7,), (15,)),
                8: ((12,), (16,)),
                9: ((9, 6, 11, 8, 13, 14, 15, 16), ()),
            }[s]
        self.landed(p, *waits)
        self.start(p, *starts)


def norm_rows(rows, gain, start, count):
    def step(i, carry):
        at = pl.ds(pl.multiple_of(start + i * 16, 16), 16)
        looked = rows[at, :].astype(F32)
        mean_sq = jnp.mean(looked * looked, axis=-1, keepdims=True)
        looked = rows[at, :].astype(F32)
        rows[at, :] = (looked * lax.rsqrt(mean_sq + norm_eps) * gain[...]).astype(BF)
        return carry

    lax.fori_loop(0, count // 16, step, 0)


def turn_rows(rows, rows_t, start, count):
    def step(j, carry):
        at = pl.multiple_of((start + j) * 128, 128)
        rows_t[pl.ds(at, 128), :] = rows[:, pl.ds(at, 128)].T
        return carry

    lax.fori_loop(0, count, step, 0)


def project(rows, w8, acc, kv, h):
    inv_root = D ** (-0.5)

    def step(i, carry):
        at = pl.multiple_of(i * 1280, 1280)
        y, x = i // 2, 2 * lax.rem(i, 2)
        pair = [w8[2 * h + e, y, pl.ds(x, 2)].reshape(1280, 128) for e in range(2)]
        acc[...] += jnp.dot(
            rows[:, pl.ds(at, 1280)],
            jnp.concatenate(pair, axis=1),
            preferred_element_type=F32,
        )
        return carry

    acc[...] = jnp.zeros_like(acc)
    lax.fori_loop(0, 4, step, 0)
    out = (acc[...] * inv_root).astype(BF)
    kv[:, h * 128 : h * 128 + 128] = out[:, :128]
    kv[:, 512 + h * 128 : 640 + h * 128] = out[:, 128:]


def interleave(comm, work):
    n = len(comm)
    done = 0
    for i, f in enumerate(comm):
        f()
        upto = (i + 1) * len(work) // n
        for g in work[done:upto]:
            g()
        done = upto


class Scatter(Moves):
    def __init__(self, place, g8, via, near, across, last, send, recv):
        super().__init__(place, send, recv)
        self.g8 = g8
        self.via, self.near, self.across, self.last = via, near, across, last

    def ends(self, p, k):
        pc, g = self.place, self.g8
        if k < 4:
            q, h = k // 2, k % 2
            return pc.half(g, p, q, 2, h), self.via.at[p, k], pc.dev(p, False, -1 if h else 1)
        if k < 12:
            d, q, h = (k - 4) // 4, (k - 4) // 2 % 2, (k - 4) % 2
            off = -1 if d else 1
            return pc.half(g, p, q, off, h), self.near.at[p, k - 4], pc.dev(p, False, off)
        if k < 14:
            return pc.half(g, p, 1, 0, k - 12), self.across.at[p, k - 12], {"lo": pc.yo}
        block = pc.block(g, p, (2, 1, -1)[k - 14])
        return block, self.last.at[p, k - 14], pc.dev(p, True, (up(p), 1, -1)[k - 14])

    def add(self, dst, *terms):
        total = dst[...].astype(F32)
        for t in terms:
            total = total + t[...].astype(F32)
        dst[...] = total.astype(BF)

    def add_half(self, dst, *terms):
        for i in range(2):
            self.add(dst.at[i], *[t.at[i] for t in terms])

    def act(self, p, s):
        pc, g, via, near = self.place, self.g8, self.via, self.near
        if s == 0:
            self.start(p, 3, 2, 7, 10)
        elif s == 1:
            self.start(p, 1, 0, 5, 8)
        elif s in (2, 3, 6, 7):
            q, h = (1 if s < 4 else 0), 1 - s % 2
            self.landed(p, 2 * q + h)
            self.add_half(pc.half(g, p, q, -1 if h else 1, h), via.at[p, 2 * q + h])
            self.start(p, 4 + h * 4 + q * 2 + h)
        elif s in (4, 5):
            h = 5 - s
            self.landed(p, 6 + h, 10 + h)
            self.add_half(pc.half(g, p, 1, 0, h), near.at[p, 2 + h], near.at[p, 6 + h])
            self.start(p, 12 + h)
        elif s in (8, 9):
            h = 9 - s
            self.landed(p, 4 + h, 8 + h, 12 + h)
            self.add_half(
                pc.half(g, p, 0, 0, h), near.at[p, h], near.at[p, 4 + h], self.across.at[p, h]
            )
            self.start(p, 14 if s == 8 else (16 if up(p) > 0 else 15))
        elif s == 10:
            self.landed(p, 14)
            self.add(pc.block(g, p, up(p)), self.last.at[p, 0])
            self.start(p, 15 if up(p) > 0 else 16)

    def total(self, p):
        self.landed(p, 15, 16)
        own = self.place.block(self.g8, p, 0)[...].astype(F32)
        return own + self.last[p, 1].astype(F32) + self.last[p, 2].astype(F32)


class Outer:
    def __init__(self, w, outer, fresh, coded, scales, mine, send, recv):
        self.hi, self.core = lax.axis_index("hi"), lax.axis_index("core")
        self.w, self.outer, self.fresh = w, outer, fresh
        self.coded, self.scales, self.mine = coded, scales, mine
        self.send, self.recv = send, recv

    def slot(self, flip_hi, flip_core):
        hi = 1 - self.hi if flip_hi else self.hi
        core = 1 - self.core if flip_core else self.core
        return hi * 2 + core

    def copy(self, p, k, arriving):
        buf = self.scales if p == 8 else self.coded
        if arriving:
            s = (self.slot(True, False), self.slot(False, True), self.slot(True, True))[k]
        else:
            s = self.slot(k == 2 and p not in DIRECT, False)
        ref = buf.at[s] if p == 8 else buf.at[s, p]
        dev = {"hi": 1 - self.hi} if k == 0 else {"core": 1 - self.core}
        if k == 2 and p in DIRECT:
            dev["hi"] = 1 - self.hi
        return remote(ref, ref, self.send.at[p, k], self.recv.at[p, k], dev)

    def share(self, p):
        for k in (0, 2, 1) if p in DIRECT else (0, 1):
            self.copy(p, k, False).start()

    def code(self, p, grad):
        c = piece_cols(p)
        cols = slice(c, c + 128)
        fresh = self.w[:, cols].astype(F32) - inner_rate * grad
        self.fresh[:, cols] = fresh
        delta = self.outer[:, cols] - fresh
        scale = (jnp.max(jnp.abs(delta), axis=1, keepdims=True) + scale_eps).astype(BF)
        scale = scale.astype(F32)
        self.coded[self.slot(False, False), p] = (delta / scale).astype(BF)
        lane = lax.broadcasted_iota(jnp.int32, self.mine.shape, 1)
        self.mine[...] = jnp.where(lane == p, scale, self.mine[...])
        self.share(p)

    def send_scales(self):
        self.scales[self.slot(False, False)] = self.mine[...].astype(BF)
        self.share(8)

    def forward(self, p):
        self.copy(p, 0, True).wait_recv()
        self.copy(p, 2, False).start()

    def arrived(self, p):
        if p in DIRECT:
            self.copy(p, 0, True).wait_recv()
        self.copy(p, 1, True).wait_recv()
        self.copy(p, 2, True).wait_recv()

    def finish(self, p, average):
        c = piece_cols(p)
        total = jnp.zeros((ROWS, 128), F32)
        for g in range(4):
            total = total + self.coded[g, p].astype(F32) * self.scales[g][:, p : p + 1].astype(F32)
        average[:, c : c + 128] = total / 4

    def drain(self):
        for p in range(9):
            for k in range(3):
                self.copy(p, k, False).wait_send()


def dot_nt(a, b):
    return lax.dot_general(a, b, (((1,), (1,)), ((), ())), preferred_element_type=F32)


def attend_back(q, og, kv, kvg, prob, cot, h, s):
    tok = slice(s * 256, s * 256 + 256)
    key = kv[tok, h * 128 : h * 128 + 128]
    val = kv[tok, 512 + h * 128 : 640 + h * 128]
    root = HD ** (-0.5)

    def one(r, carry):
        at = pl.multiple_of((h * 5 + r) * 128, 128)
        for b in range(2):
            m = 128 * (b + 1)
            rows = pl.ds(s * 256 + b * 128, 128)
            qb, gb = q[rows, pl.ds(at, 128)], og[rows, pl.ds(at, 128)]
            sc = dot_nt(key[:m], qb) * root
            keys = lax.broadcasted_iota(jnp.int32, (m, 128), 0)
            places = lax.broadcasted_iota(jnp.int32, (m, 128), 1) + b * 128
            sc = jnp.where(keys <= places, sc, -1e30)
            ex = jnp.exp(sc - jnp.max(sc, axis=0, keepdims=True))
            pr = ex * (1.0 / jnp.sum(ex, axis=0, keepdims=True))
            dp = dot_nt(val[:m], gb).astype(BF).astype(F32)
            prod = pr * dp
            ds = prod - pr * jnp.sum(prod, axis=0, keepdims=True)
            to = pl.ds(pl.multiple_of(r * 256 + b * 128, 128), 128)
            prob[:m, to] = pr.astype(BF)
            cot[:m, to] = ds.astype(BF)
        return carry

    lax.fori_loop(0, 5, one, 0, unroll=UNROLL)
    base = h * 640
    rows = slice(s * 256, s * 256 + 256)
    stack = lambda ref: jnp.concatenate(
        [ref[rows, base + r * 128 : base + r * 128 + 128] for r in range(5)], axis=0
    )
    dk = jnp.dot(cot[...], stack(q), preferred_element_type=F32) * root
    dv = jnp.dot(prob[...], stack(og), preferred_element_type=F32)
    kvg[h, tok, :128] = dk.astype(BF)
    kvg[h, tok, 128:] = dv.astype(BF)


UNROLL = 5


def grad_rows(rows_t, kvg, g8, h, y):
    inv_root = D ** (-0.5)

    def one(x, carry):
        at = pl.multiple_of((y * 4 + x) * 640, 640)
        out = jnp.dot(rows_t[pl.ds(at, 640), :], kvg[h], preferred_element_type=F32) * inv_root
        out = out.astype(BF)
        g8[2 * h, y, x] = out[:, :128].reshape(4, ROWS, 128)
        g8[2 * h + 1, y, x] = out[:, 128:].reshape(4, ROWS, 128)
        return carry

    lax.fori_loop(0, 4, one, 0)


def step_kernel(
    hidden, gain_any, w_any, q_any, og_any, outer_any,
    fresh, average,
    gain, w, outer, q, og, rows, rows_t, w8, acc, kv, kvg, prob, cot,
    g8, via, near, across, last, coded, scales, mine,
    ag_send, ag_recv, send, recv, x_send, x_recv, load_sem, own_sem, arg_sem,
):
    pc = Place()
    ga = Gather(pc, w8, ag_send, ag_recv)
    sc = Scatter(pc, g8, via, near, across, last, send, recv)
    ex = Outer(w, outer, fresh, coded, scales, mine, x_send, x_recv)
    owns = []
    for p in range(8):
        c = piece_cols(p)
        owns.append(
            pltpu.make_async_copy(
                w_any.at[:, c : c + 128], pc.block(w8, p, 0), own_sem.at[p]
            )
        )
    loads = []
    for i in range(8):
        at = slice(i * 64, i * 64 + 64)
        loads.append(pltpu.make_async_copy(hidden.at[at], rows.at[at], load_sem.at[i]))
    args = [
        pltpu.make_async_copy(a, b, arg_sem.at[i])
        for i, (a, b) in enumerate(
            (
                (gain_any, gain),
                (q_any, q),
                (og_any, og),
                (w_any, w),
                (outer_any, outer),
            )
        )
    ]
    for cp in owns + args[:1] + loads + args[1:]:
        cp.start()
    meet(
        [{"lo": pc.yo}, {"hi": 1 - ex.hi}, {"core": 1 - ex.core}]
        + [{"hi": 1 - ex.hi, "core": 1 - ex.core}]
        + [pc.dev(p, True, o) for p in range(2) for o in (1, -1)]
    )
    for p in range(8):
        owns[p].wait()
    args[0].wait()

    def norm(i):
        loads[i].wait()
        norm_rows(rows, gain, i * 64, 64)

    def turn(i):
        turn_rows(rows, rows_t, i * 5, 5)

    def scatter(p, s):
        if s < 11:
            sc.act(p, s)
        elif s == 11:
            ex.code(p, sc.total(p))
        else:
            ex.forward(p)

    def attn(h, s):
        attend_back(q, og, kv, kvg, prob, cot, h, s)

    def grads(h, near):
        grad_rows(rows_t, kvg, g8, h, pc.plane(1 - near))

    def proj(h):
        project(rows, w8, acc, kv, h)

    def clear():
        prob[...] = jnp.zeros_like(prob)
        cot[...] = jnp.zeros_like(cot)
        mine[...] = jnp.zeros_like(mine)
        for cp in args[1:]:
            cp.wait()

    acts = dict(G=ga.act, T=scatter, A=attn, M=grads, P=proj, N=norm, U=turn, C=clear)
    for kind, *nums in ORDER:
        acts[kind](*nums)
    ex.send_scales()
    for p in range(8):
        ex.arrived(p)
    ex.arrived(8)
    for p in range(8):
        ex.finish(p, average)
    ga.drain()
    sc.drain()
    ex.drain()


LATE_Y = (4, 5,)

DIRECT = (6, 7, 8)

ORDER = (
    ("G", 1, 0), ("G", 0, 0), ("G", 3, 0), ("G", 2, 0), ("G", 4, 0), ("G", 5, 0), ("C",),
    ("G", 6, 0), ("N", 0), ("N", 1), ("G", 1, 1), ("G", 0, 1), ("N", 2), ("G", 3, 1), ("G", 2, 1),
    ("N", 3), ("G", 1, 2), ("G", 7, 0), ("N", 4), ("G", 1, 3), ("N", 5), ("G", 1, 5), ("G", 0, 2),
    ("G", 0, 5), ("N", 6), ("G", 0, 3), ("G", 2, 5), ("G", 3, 2), ("N", 7), ("G", 3, 3),
    ("G", 2, 2), ("U", 0), ("U", 7), ("G", 1, 6), ("U", 4), ("G", 0, 6), ("G", 2, 3), ("G", 3, 5),
    ("U", 3), ("U", 1), ("U", 5), ("G", 1, 7), ("G", 6, 1), ("U", 2), ("U", 6), ("G", 1, 4),
    ("G", 3, 6), ("G", 2, 6), ("G", 0, 7), ("G", 3, 4), ("G", 0, 4), ("G", 3, 7), ("G", 2, 4),
    ("G", 7, 1), ("G", 2, 7), ("G", 1, 8), ("G", 5, 1), ("G", 6, 5), ("G", 7, 3), ("G", 0, 8),
    ("G", 3, 8), ("G", 6, 3), ("G", 2, 8), ("G", 7, 2), ("G", 6, 2), ("G", 1, 9), ("G", 0, 9),
    ("G", 4, 1), ("G", 7, 5), ("P", 0), ("G", 5, 2), ("G", 5, 5), ("A", 0, 0), ("G", 2, 9),
    ("G", 5, 3), ("G", 6, 4), ("A", 0, 1), ("G", 3, 9), ("G", 7, 4), ("G", 6, 7), ("G", 6, 6),
    ("M", 0, 0), ("G", 4, 5), ("G", 4, 2), ("G", 7, 6), ("G", 7, 7), ("T", 0, 0), ("M", 0, 1),
    ("G", 5, 4), ("G", 6, 8), ("T", 1, 0), ("P", 1), ("G", 4, 3), ("G", 5, 6), ("G", 7, 8),
    ("A", 1, 0), ("G", 4, 4), ("T", 1, 1), ("T", 0, 1), ("A", 1, 1), ("G", 5, 8), ("M", 1, 0),
    ("G", 4, 6), ("T", 0, 2), ("T", 1, 2), ("T", 0, 3), ("M", 1, 1), ("G", 5, 7), ("T", 1, 3),
    ("G", 6, 9), ("T", 3, 0), ("T", 2, 0), ("G", 7, 9), ("P", 3), ("G", 4, 8), ("T", 1, 7),
    ("T", 0, 7), ("T", 1, 6), ("A", 3, 0), ("G", 4, 7), ("T", 0, 6), ("T", 3, 1), ("A", 3, 1),
    ("T", 1, 5), ("T", 2, 1), ("M", 3, 0), ("T", 0, 4), ("M", 3, 1), ("G", 5, 9), ("T", 0, 5),
    ("T", 3, 2), ("T", 3, 3), ("T", 2, 3), ("T", 2, 2), ("T", 7, 0), ("T", 6, 0), ("T", 1, 4),
    ("G", 4, 9), ("P", 2), ("T", 2, 7), ("T", 2, 6), ("T", 3, 7), ("T", 3, 6), ("A", 2, 0),
    ("T", 0, 8), ("T", 6, 1), ("A", 2, 1), ("T", 0, 9), ("T", 2, 4), ("T", 2, 5), ("T", 3, 4),
    ("M", 2, 0), ("T", 1, 8), ("T", 3, 5), ("T", 1, 9), ("T", 7, 2), ("T", 7, 3), ("T", 5, 0),
    ("T", 6, 3), ("M", 2, 1), ("T", 6, 2), ("T", 5, 1), ("T", 4, 0), ("T", 7, 5), ("T", 7, 4),
    ("T", 0, 10), ("T", 2, 8), ("T", 6, 7), ("T", 3, 8), ("T", 2, 9), ("T", 5, 2), ("T", 6, 6),
    ("T", 5, 3), ("T", 1, 10), ("T", 3, 9), ("T", 6, 5), ("T", 7, 1), ("T", 6, 4), ("T", 4, 1),
    ("T", 5, 6), ("T", 4, 2), ("T", 5, 7), ("T", 4, 3), ("T", 0, 11), ("T", 2, 10), ("T", 3, 10),
    ("T", 5, 4), ("T", 1, 11), ("T", 6, 8), ("T", 6, 9), ("T", 5, 5), ("T", 7, 6), ("T", 4, 6),
    ("T", 7, 7), ("T", 4, 7), ("T", 0, 12), ("T", 5, 8), ("T", 4, 4), ("T", 2, 11), ("T", 5, 9),
    ("T", 4, 5), ("T", 3, 11), ("T", 6, 10), ("T", 1, 12), ("T", 7, 8), ("T", 7, 9), ("T", 5, 10),
    ("T", 4, 8), ("T", 6, 11), ("T", 7, 10), ("T", 4, 9), ("T", 4, 10), ("T", 5, 11), ("T", 2, 12),
    ("T", 7, 11), ("T", 4, 11), ("T", 3, 12), ("T", 5, 12), ("T", 4, 12),
)


def step(*arrays):
    hbm, vm = pl.BlockSpec(memory_space=pl.ANY), pl.BlockSpec(memory_space=pltpu.VMEM)
    return pl.pallas_call(
        step_kernel,
        out_shape=(
            jax.ShapeDtypeStruct((ROWS, KVC), F32),
            jax.ShapeDtypeStruct((ROWS, KVC), F32),
        ),
        in_specs=[hbm] * 6,
        out_specs=(vm, vm),
        scratch_shapes=[
            pltpu.VMEM((1, D), F32),
            pltpu.VMEM((ROWS, KVC), BF),
            pltpu.VMEM((ROWS, KVC), F32),
            pltpu.VMEM((TOK, 2560), BF),
            pltpu.VMEM((TOK, 2560), BF),
            pltpu.VMEM((TOK, D), BF),
            pltpu.VMEM((D, TOK), BF),
            pltpu.VMEM((8, 2, 4, 4, ROWS, 128), BF),
            pltpu.VMEM((TOK, 256), F32),
            pltpu.VMEM((TOK, KVC), BF),
            pltpu.VMEM((4, TOK, 256), BF),
            pltpu.VMEM((256, 1280), BF),
            pltpu.VMEM((256, 1280), BF),
            pltpu.VMEM((8, 2, 4, 4, ROWS, 128), BF),
            pltpu.VMEM((8, 4, 2, ROWS, 128), BF),
            pltpu.VMEM((8, 8, 2, ROWS, 128), BF),
            pltpu.VMEM((8, 2, 2, ROWS, 128), BF),
            pltpu.VMEM((8, 3, ROWS, 128), BF),
            pltpu.VMEM((4, 8, ROWS, 128), BF),
            pltpu.VMEM((4, ROWS, 128), BF),
            pltpu.VMEM((ROWS, 128), F32),
            pltpu.SemaphoreType.DMA((8, 17)),
            pltpu.SemaphoreType.DMA((8, 17)),
            pltpu.SemaphoreType.DMA((8, 17)),
            pltpu.SemaphoreType.DMA((8, 17)),
            pltpu.SemaphoreType.DMA((9, 3)),
            pltpu.SemaphoreType.DMA((9, 3)),
            pltpu.SemaphoreType.DMA((8,)),
            pltpu.SemaphoreType.DMA((8,)),
            pltpu.SemaphoreType.DMA((5,)),
        ],
        compiler_params=pltpu.CompilerParams(
            collective_id=0, has_side_effects=True, vmem_limit_bytes=67043328
        ),
    )(*arrays)


def local(hidden, norm_gain, queries, out_grad, kv_inner, kv_outer, momentum):
    fresh, average = step(
        hidden[0].reshape(TOK, D),
        norm_gain.reshape(1, D),
        kv_inner[0],
        queries[0].reshape(TOK, -1),
        out_grad[0].reshape(TOK, -1),
        kv_outer,
    )
    moment_new = momentum_decay * momentum + average
    outer_new = kv_outer - outer_rate * (momentum_decay * moment_new + average)
    blended = (blend_share * fresh + (1.0 - blend_share) * outer_new).astype(BF)
    return (blended[None], outer_new, moment_new)


def solution(mesh):
    split = Mesh(
        mesh.devices.reshape(2, 2, 2, 4, 4), GROUP + FSDP
    )
    return jax.shard_map(
        local,
        mesh=split,
        in_specs=(
            P(GROUP, FSDP, None, None),
            P(),
            P(GROUP, FSDP, None, None),
            P(GROUP, FSDP, None, None),
            P(GROUP, FSDP, None),
            P(FSDP, None),
            P(FSDP, None),
        ),
        out_specs=(P(GROUP, FSDP, None), P(FSDP, None), P(FSDP, None)),
        check_vma=False,
    )
```

```python
import functools
import jax
import jax.numpy as jnp
from jax import lax
from jax.experimental import pallas as pl
from jax.experimental.pallas import tpu as pltpu
from jax.sharding import Mesh
from jax.sharding import PartitionSpec as P

D = 5120
HD = 128
KVC = 1024
TOK = 512
ROWS = 160
QBLOCK = 128
GROUP = ("hi", "core")
FSDP = ("lo", "x", "z")
MESH = pl.DeviceIdType.MESH
BF = jnp.bfloat16
F32 = jnp.float32


inner_rate = 0.25
outer_rate = 0.7
momentum_decay = 0.9
blend_share = 0.5
norm_eps = 1e-06
scale_eps = 1e-06


def piece_cols(p):
    return (p // 2) * 128 + (p % 2) * 512


class Place:
    def __init__(self):
        self.y = lax.axis_index("lo")
        self.x = lax.axis_index("x")
        self.z = lax.axis_index("z")
        self.yo = 1 - self.y

    def names(self, p):
        return ("x", "z") if p % 2 == 0 else ("z", "x")

    def at(self, p, first, off):
        v = getattr(self, self.names(p)[0 if first else 1])
        return lax.rem(v + (off + 4), 4)

    def dev(self, p, first, off):
        return {self.names(p)[0 if first else 1]: self.at(p, first, off)}

    def plane(self, q):
        return self.yo if q else self.y

    def half(self, ref, p, q, c_off, h):
        c = self.at(p, False, c_off)
        low = 2 * (self.at(p, True, 0) // 2)
        two = pl.ds(2 - low if h else low, 2)
        if p % 2 == 0:
            return ref.at[p, self.plane(q), two, c]
        return ref.at[p, self.plane(q), c, two]

    def block(self, ref, p, a_off):
        a, c = self.at(p, True, a_off), self.at(p, False, 0)
        if p % 2 == 0:
            return ref.at[p, self.y, a, c]
        return ref.at[p, self.y, c, a]


def remote(src, dst, send, recv, dev):
    return pltpu.make_async_remote_copy(
        src_ref=src, dst_ref=dst, send_sem=send, recv_sem=recv, device_id=dev, device_id_type=MESH
    )


def meet(devs):
    barrier = pltpu.get_barrier_semaphore()
    for dev in devs:
        pl.semaphore_signal(barrier, inc=1, device_id=dev, device_id_type=MESH)
    pl.semaphore_wait(barrier, len(devs))


def up(p):
    return 1 if (p // 2) % 2 == 0 else -1


class Moves:
    def __init__(self, place, send, recv):
        self.place, self.send, self.recv, self.used = place, send, recv, []

    def copy(self, p, k):
        src, dst, dev = self.ends(p, k)
        return remote(src, dst, self.send.at[p, k], self.recv.at[p, k], dev)

    def start(self, p, *keys):
        for k in keys:
            self.copy(p, k).start()
            self.used.append((p, k))

    def landed(self, p, *keys):
        for k in keys:
            self.copy(p, k).wait_recv()

    def drain(self):
        for p, k in self.used:
            self.copy(p, k).wait_send()


class Gather(Moves):
    def __init__(self, place, w8, send, recv):
        super().__init__(place, send, recv)
        self.w8 = w8

    def ends(self, p, k):
        pc, w = self.place, self.w8
        if k < 3:
            src = pc.block(w, p, (0, 0, -up(p))[k])
            return src, src, pc.dev(p, True, (1, -1, up(p))[k])
        if p in LATE_Y:
            if k < 5:
                h = k - 3
                src, dev = pc.half(w, p, 0, 1 if h else -1, h), pc.dev(p, False, -1 if h else 1)
            elif k < 9:
                d, h = (k - 5) // 2, (k - 5) % 2
                src, dev = pc.half(w, p, 0, 0, h), pc.dev(p, False, -1 if d else 1)
            else:
                c, h = (k - 9) // 2, (k - 9) % 2
                src, dev = pc.half(w, p, 0, (0, -1, 1, 2)[c], h), {"lo": pc.yo}
        elif k < 5:
            src, dev = pc.half(w, p, 0, 0, k - 3), {"lo": pc.yo}
        elif k < 13:
            d, q, h = (k - 5) // 4, (k - 5) // 2 % 2, (k - 5) % 2
            src, dev = pc.half(w, p, q, 0, h), pc.dev(p, False, -1 if d else 1)
        else:
            q, h = (k - 13) // 2, (k - 13) % 2
            src, dev = pc.half(w, p, q, 1 if h else -1, h), pc.dev(p, False, -1 if h else 1)
        return src, src, dev

    def act(self, p, s):
        if p in LATE_Y:
            waits, starts = {
                0: ((), (0, 1)),
                1: ((0, 1), (2, 5, 7, 9)),
                2: ((2,), (8, 6, 10)),
                3: ((5,), (3, 11)),
                4: ((8,), (4, 14)),
                5: ((7,), (13,)),
                6: ((6,), (12,)),
                7: ((3,), (15,)),
                8: ((4,), (16,)),
                9: (tuple(range(9, 17)), ()),
            }[s]
        else:
            waits, starts = {
                0: ((), (0, 1)),
                1: ((0, 1), (2, 3, 5, 9)),
                2: ((2,), (4, 10, 6)),
                3: ((3,), (7, 11)),
                4: ((4,), (12, 8)),
                5: ((5,), (13,)),
                6: ((10,), (14,)),
                7: ((7,), (15,)),
                8: ((12,), (16,)),
                9: ((9, 6, 11, 8, 13, 14, 15, 16), ()),
            }[s]
        self.landed(p, *waits)
        self.start(p, *starts)


def norm_rows(rows, gain, start, count):
    def step(i, carry):
        at = pl.ds(pl.multiple_of(start + i * 16, 16), 16)
        looked = rows[at, :].astype(F32)
        mean_sq = jnp.mean(looked * looked, axis=-1, keepdims=True)
        looked = rows[at, :].astype(F32)
        rows[at, :] = (looked * lax.rsqrt(mean_sq + norm_eps) * gain[...]).astype(BF)
        return carry

    lax.fori_loop(0, count // 16, step, 0)


def turn_rows(rows, rows_t, start, count):
    def step(j, carry):
        at = pl.multiple_of((start + j) * 128, 128)
        rows_t[pl.ds(at, 128), :] = rows[:, pl.ds(at, 128)].T
        return carry

    lax.fori_loop(0, count, step, 0)


def project(rows, w8, acc, kv, h):
    inv_root = D ** (-0.5)

    def step(i, carry):
        at = pl.multiple_of(i * 1280, 1280)
        y, x = i // 2, 2 * lax.rem(i, 2)
        pair = [w8[2 * h + e, y, pl.ds(x, 2)].reshape(1280, 128) for e in range(2)]
        acc[...] += jnp.dot(
            rows[:, pl.ds(at, 1280)],
            jnp.concatenate(pair, axis=1),
            preferred_element_type=F32,
        )
        return carry

    acc[...] = jnp.zeros_like(acc)
    lax.fori_loop(0, 4, step, 0)
    out = (acc[...] * inv_root).astype(BF)
    kv[:, h * 128 : h * 128 + 128] = out[:, :128]
    kv[:, 512 + h * 128 : 640 + h * 128] = out[:, 128:]


def interleave(comm, work):
    n = len(comm)
    done = 0
    for i, f in enumerate(comm):
        f()
        upto = (i + 1) * len(work) // n
        for g in work[done:upto]:
            g()
        done = upto


class Scatter(Moves):
    def __init__(self, place, g8, via, near, across, last, send, recv):
        super().__init__(place, send, recv)
        self.g8 = g8
        self.via, self.near, self.across, self.last = via, near, across, last

    def ends(self, p, k):
        pc, g = self.place, self.g8
        if k < 4:
            q, h = k // 2, k % 2
            return pc.half(g, p, q, 2, h), self.via.at[p, k], pc.dev(p, False, -1 if h else 1)
        if k < 12:
            d, q, h = (k - 4) // 4, (k - 4) // 2 % 2, (k - 4) % 2
            off = -1 if d else 1
            return pc.half(g, p, q, off, h), self.near.at[p, k - 4], pc.dev(p, False, off)
        if k < 14:
            return pc.half(g, p, 1, 0, k - 12), self.across.at[p, k - 12], {"lo": pc.yo}
        block = pc.block(g, p, (2, 1, -1)[k - 14])
        return block, self.last.at[p, k - 14], pc.dev(p, True, (up(p), 1, -1)[k - 14])

    def add(self, dst, *terms):
        total = dst[...].astype(F32)
        for t in terms:
            total = total + t[...].astype(F32)
        dst[...] = total.astype(BF)

    def add_half(self, dst, *terms):
        for i in range(2):
            self.add(dst.at[i], *[t.at[i] for t in terms])

    def act(self, p, s):
        pc, g, via, near = self.place, self.g8, self.via, self.near
        if s == 0:
            self.start(p, 3, 2, 7, 10)
        elif s == 1:
            self.start(p, 1, 0, 5, 8)
        elif s in (2, 3, 6, 7):
            q, h = (1 if s < 4 else 0), 1 - s % 2
            self.landed(p, 2 * q + h)
            self.add_half(pc.half(g, p, q, -1 if h else 1, h), via.at[p, 2 * q + h])
            self.start(p, 4 + h * 4 + q * 2 + h)
        elif s in (4, 5):
            h = 5 - s
            self.landed(p, 6 + h, 10 + h)
            self.add_half(pc.half(g, p, 1, 0, h), near.at[p, 2 + h], near.at[p, 6 + h])
            self.start(p, 12 + h)
        elif s in (8, 9):
            h = 9 - s
            self.landed(p, 4 + h, 8 + h, 12 + h)
            self.add_half(
                pc.half(g, p, 0, 0, h), near.at[p, h], near.at[p, 4 + h], self.across.at[p, h]
            )
            self.start(p, 14 if s == 8 else (16 if up(p) > 0 else 15))
        elif s == 10:
            self.landed(p, 14)
            self.add(pc.block(g, p, up(p)), self.last.at[p, 0])
            self.start(p, 15 if up(p) > 0 else 16)

    def total(self, p):
        self.landed(p, 15, 16)
        own = self.place.block(self.g8, p, 0)[...].astype(F32)
        return own + self.last[p, 1].astype(F32) + self.last[p, 2].astype(F32)


class Outer:
    def __init__(self, w, outer, fresh, coded, scales, mine, send, recv):
        self.hi, self.core = lax.axis_index("hi"), lax.axis_index("core")
        self.w, self.outer, self.fresh = w, outer, fresh
        self.coded, self.scales, self.mine = coded, scales, mine
        self.send, self.recv = send, recv

    def slot(self, flip_hi, flip_core):
        hi = 1 - self.hi if flip_hi else self.hi
        core = 1 - self.core if flip_core else self.core
        return hi * 2 + core

    def copy(self, p, k, arriving):
        buf = self.scales if p == 8 else self.coded
        if arriving:
            s = (self.slot(True, False), self.slot(False, True), self.slot(True, True))[k]
        else:
            s = self.slot(k == 2 and p not in DIRECT, False)
        ref = buf.at[s] if p == 8 else buf.at[s, p]
        dev = {"hi": 1 - self.hi} if k == 0 else {"core": 1 - self.core}
        if k == 2 and p in DIRECT:
            dev["hi"] = 1 - self.hi
        return remote(ref, ref, self.send.at[p, k], self.recv.at[p, k], dev)

    def share(self, p):
        for k in (0, 2, 1) if p in DIRECT else (0, 1):
            self.copy(p, k, False).start()

    def code(self, p, grad):
        c = piece_cols(p)
        cols = slice(c, c + 128)
        fresh = self.w[:, cols].astype(F32) - inner_rate * grad
        self.fresh[:, cols] = fresh
        delta = self.outer[:, cols] - fresh
        scale = (jnp.max(jnp.abs(delta), axis=1, keepdims=True) + scale_eps).astype(BF)
        scale = scale.astype(F32)
        self.coded[self.slot(False, False), p] = (delta / scale).astype(BF)
        lane = lax.broadcasted_iota(jnp.int32, self.mine.shape, 1)
        self.mine[...] = jnp.where(lane == p, scale, self.mine[...])
        self.share(p)

    def send_scales(self):
        self.scales[self.slot(False, False)] = self.mine[...].astype(BF)
        self.share(8)

    def forward(self, p):
        self.copy(p, 0, True).wait_recv()
        self.copy(p, 2, False).start()

    def arrived(self, p):
        if p in DIRECT:
            self.copy(p, 0, True).wait_recv()
        self.copy(p, 1, True).wait_recv()
        self.copy(p, 2, True).wait_recv()

    def finish(self, p, average):
        c = piece_cols(p)
        total = jnp.zeros((ROWS, 128), F32)
        for g in range(4):
            total = total + self.coded[g, p].astype(F32) * self.scales[g][:, p : p + 1].astype(F32)
        average[:, c : c + 128] = total / 4

    def drain(self):
        for p in range(9):
            for k in range(3):
                self.copy(p, k, False).wait_send()


def dot_nt(a, b):
    return lax.dot_general(a, b, (((1,), (1,)), ((), ())), preferred_element_type=F32)


def attend_back(q, og, kv, kvg, prob, cot, h, s):
    tok = slice(s * 256, s * 256 + 256)
    key = kv[tok, h * 128 : h * 128 + 128]
    val = kv[tok, 512 + h * 128 : 640 + h * 128]
    root = HD ** (-0.5)

    def one(r, carry):
        at = pl.multiple_of((h * 5 + r) * 128, 128)
        for b in range(2):
            m = 128 * (b + 1)
            rows = pl.ds(s * 256 + b * 128, 128)
            qb, gb = q[rows, pl.ds(at, 128)], og[rows, pl.ds(at, 128)]
            sc = dot_nt(key[:m], qb) * root
            keys = lax.broadcasted_iota(jnp.int32, (m, 128), 0)
            places = lax.broadcasted_iota(jnp.int32, (m, 128), 1) + b * 128
            sc = jnp.where(keys <= places, sc, -1e30)
            ex = jnp.exp(sc - jnp.max(sc, axis=0, keepdims=True))
            pr = ex * (1.0 / jnp.sum(ex, axis=0, keepdims=True))
            dp = dot_nt(val[:m], gb).astype(BF).astype(F32)
            prod = pr * dp
            ds = prod - pr * jnp.sum(prod, axis=0, keepdims=True)
            to = pl.ds(pl.multiple_of(r * 256 + b * 128, 128), 128)
            prob[:m, to] = pr.astype(BF)
            cot[:m, to] = ds.astype(BF)
        return carry

    lax.fori_loop(0, 5, one, 0, unroll=UNROLL)
    base = h * 640
    rows = slice(s * 256, s * 256 + 256)
    stack = lambda ref: jnp.concatenate(
        [ref[rows, base + r * 128 : base + r * 128 + 128] for r in range(5)], axis=0
    )
    dk = jnp.dot(cot[...], stack(q), preferred_element_type=F32) * root
    dv = jnp.dot(prob[...], stack(og), preferred_element_type=F32)
    kvg[h, tok, :128] = dk.astype(BF)
    kvg[h, tok, 128:] = dv.astype(BF)


UNROLL = 5


def grad_rows(rows_t, kvg, g8, h, y):
    inv_root = D ** (-0.5)

    def one(x, carry):
        at = pl.multiple_of((y * 4 + x) * 640, 640)
        out = jnp.dot(rows_t[pl.ds(at, 640), :], kvg[h], preferred_element_type=F32) * inv_root
        out = out.astype(BF)
        g8[2 * h, y, x] = out[:, :128].reshape(4, ROWS, 128)
        g8[2 * h + 1, y, x] = out[:, 128:].reshape(4, ROWS, 128)
        return carry

    lax.fori_loop(0, 4, one, 0)


def step_kernel(
    hidden, gain_any, w_any, q_any, og_any, outer_any,
    fresh, average,
    gain, w, outer, q, og, rows, rows_t, w8, acc, kv, kvg, prob, cot,
    g8, via, near, across, last, coded, scales, mine,
    ag_send, ag_recv, send, recv, x_send, x_recv, load_sem, own_sem, arg_sem,
):
    pc = Place()
    ga = Gather(pc, w8, ag_send, ag_recv)
    sc = Scatter(pc, g8, via, near, across, last, send, recv)
    ex = Outer(w, outer, fresh, coded, scales, mine, x_send, x_recv)
    owns = []
    for p in range(8):
        c = piece_cols(p)
        owns.append(
            pltpu.make_async_copy(
                w_any.at[:, c : c + 128], pc.block(w8, p, 0), own_sem.at[p]
            )
        )
    loads = []
    for i in range(8):
        at = slice(i * 64, i * 64 + 64)
        loads.append(pltpu.make_async_copy(hidden.at[at], rows.at[at], load_sem.at[i]))
    args = [
        pltpu.make_async_copy(a, b, arg_sem.at[i])
        for i, (a, b) in enumerate(
            (
                (gain_any, gain),
                (q_any, q),
                (og_any, og),
                (w_any, w),
                (outer_any, outer),
            )
        )
    ]
    for cp in owns + args[:1] + loads + args[1:]:
        cp.start()
    meet(
        [{"lo": pc.yo}, {"hi": 1 - ex.hi}, {"core": 1 - ex.core}]
        + [{"hi": 1 - ex.hi, "core": 1 - ex.core}]
        + [pc.dev(p, True, o) for p in range(2) for o in (1, -1)]
    )
    for p in range(8):
        owns[p].wait()
    args[0].wait()

    def norm(i):
        loads[i].wait()
        norm_rows(rows, gain, i * 64, 64)

    def turn(i):
        turn_rows(rows, rows_t, i * 5, 5)

    def scatter(p, s):
        if s < 11:
            sc.act(p, s)
        elif s == 11:
            ex.code(p, sc.total(p))
        else:
            ex.forward(p)

    def attn(h, s):
        attend_back(q, og, kv, kvg, prob, cot, h, s)

    def grads(h, near):
        grad_rows(rows_t, kvg, g8, h, pc.plane(1 - near))

    def proj(h):
        project(rows, w8, acc, kv, h)

    def clear():
        prob[...] = jnp.zeros_like(prob)
        cot[...] = jnp.zeros_like(cot)
        mine[...] = jnp.zeros_like(mine)
        for cp in args[1:]:
            cp.wait()

    acts = dict(G=ga.act, T=scatter, A=attn, M=grads, P=proj, N=norm, U=turn, C=clear)
    for kind, *nums in ORDER:
        acts[kind](*nums)
    ex.send_scales()
    for p in range(8):
        ex.arrived(p)
    ex.arrived(8)
    for p in range(8):
        ex.finish(p, average)
    ga.drain()
    sc.drain()
    ex.drain()


LATE_Y = (4, 5,)

DIRECT = (6, 7, 8)

ORDER = (
    ("G", 1, 0), ("G", 0, 0), ("G", 3, 0), ("G", 2, 0), ("G", 4, 0), ("G", 5, 0), ("C",),
    ("G", 6, 0), ("N", 0), ("N", 1), ("G", 1, 1), ("G", 0, 1), ("N", 2), ("G", 3, 1), ("G", 2, 1),
    ("N", 3), ("G", 1, 2), ("G", 7, 0), ("N", 4), ("G", 1, 3), ("N", 5), ("G", 1, 5), ("G", 0, 2),
    ("G", 0, 5), ("N", 6), ("G", 0, 3), ("G", 2, 5), ("G", 3, 2), ("N", 7), ("G", 3, 3),
    ("G", 2, 2), ("U", 0), ("U", 7), ("G", 1, 6), ("U", 4), ("G", 0, 6), ("G", 2, 3), ("G", 3, 5),
    ("U", 3), ("U", 1), ("U", 5), ("G", 1, 7), ("G", 6, 1), ("U", 2), ("U", 6), ("G", 1, 4),
    ("G", 3, 6), ("G", 2, 6), ("G", 0, 7), ("G", 3, 4), ("G", 0, 4), ("G", 3, 7), ("G", 2, 4),
    ("G", 7, 1), ("G", 2, 7), ("G", 1, 8), ("G", 5, 1), ("G", 6, 5), ("G", 7, 3), ("G", 0, 8),
    ("G", 3, 8), ("G", 6, 3), ("G", 2, 8), ("G", 7, 2), ("G", 6, 2), ("G", 1, 9), ("G", 0, 9),
    ("G", 4, 1), ("G", 7, 5), ("P", 0), ("G", 5, 2), ("G", 5, 5), ("A", 0, 0), ("G", 2, 9),
    ("G", 5, 3), ("G", 6, 4), ("A", 0, 1), ("G", 3, 9), ("G", 7, 4), ("G", 6, 7), ("G", 6, 6),
    ("M", 0, 0), ("G", 4, 5), ("G", 4, 2), ("G", 7, 6), ("G", 7, 7), ("T", 0, 0), ("M", 0, 1),
    ("G", 5, 4), ("G", 6, 8), ("T", 1, 0), ("P", 1), ("G", 4, 3), ("G", 5, 6), ("G", 7, 8),
    ("A", 1, 0), ("G", 4, 4), ("T", 1, 1), ("T", 0, 1), ("A", 1, 1), ("G", 5, 8), ("M", 1, 0),
    ("G", 4, 6), ("T", 0, 2), ("T", 1, 2), ("T", 0, 3), ("M", 1, 1), ("G", 5, 7), ("T", 1, 3),
    ("G", 6, 9), ("T", 3, 0), ("T", 2, 0), ("G", 7, 9), ("P", 3), ("G", 4, 8), ("T", 1, 7),
    ("T", 0, 7), ("T", 1, 6), ("A", 3, 0), ("G", 4, 7), ("T", 0, 6), ("T", 3, 1), ("A", 3, 1),
    ("T", 1, 5), ("T", 2, 1), ("M", 3, 0), ("T", 0, 4), ("M", 3, 1), ("G", 5, 9), ("T", 0, 5),
    ("T", 3, 2), ("T", 3, 3), ("T", 2, 3), ("T", 2, 2), ("T", 7, 0), ("T", 6, 0), ("T", 1, 4),
    ("G", 4, 9), ("P", 2), ("T", 2, 7), ("T", 2, 6), ("T", 3, 7), ("T", 3, 6), ("A", 2, 0),
    ("T", 0, 8), ("T", 6, 1), ("A", 2, 1), ("T", 0, 9), ("T", 2, 4), ("T", 2, 5), ("T", 3, 4),
    ("M", 2, 0), ("T", 1, 8), ("T", 3, 5), ("T", 1, 9), ("T", 7, 2), ("T", 7, 3), ("T", 5, 0),
    ("T", 6, 3), ("M", 2, 1), ("T", 6, 2), ("T", 5, 1), ("T", 4, 0), ("T", 7, 5), ("T", 7, 4),
    ("T", 0, 10), ("T", 2, 8), ("T", 6, 7), ("T", 3, 8), ("T", 2, 9), ("T", 5, 2), ("T", 6, 6),
    ("T", 5, 3), ("T", 1, 10), ("T", 3, 9), ("T", 6, 5), ("T", 7, 1), ("T", 6, 4), ("T", 4, 1),
    ("T", 5, 6), ("T", 4, 2), ("T", 5, 7), ("T", 4, 3), ("T", 0, 11), ("T", 2, 10), ("T", 3, 10),
    ("T", 5, 4), ("T", 1, 11), ("T", 6, 8), ("T", 6, 9), ("T", 5, 5), ("T", 7, 6), ("T", 4, 6),
    ("T", 7, 7), ("T", 4, 7), ("T", 0, 12), ("T", 5, 8), ("T", 4, 4), ("T", 2, 11), ("T", 5, 9),
    ("T", 4, 5), ("T", 3, 11), ("T", 6, 10), ("T", 1, 12), ("T", 7, 8), ("T", 7, 9), ("T", 5, 10),
    ("T", 4, 8), ("T", 6, 11), ("T", 7, 10), ("T", 4, 9), ("T", 4, 10), ("T", 5, 11), ("T", 2, 12),
    ("T", 7, 11), ("T", 4, 11), ("T", 3, 12), ("T", 5, 12), ("T", 4, 12),
)


def step(*arrays):
    hbm, vm = pl.BlockSpec(memory_space=pl.ANY), pl.BlockSpec(memory_space=pltpu.VMEM)
    return pl.pallas_call(
        step_kernel,
        out_shape=(
            jax.ShapeDtypeStruct((ROWS, KVC), F32),
            jax.ShapeDtypeStruct((ROWS, KVC), F32),
        ),
        in_specs=[hbm] * 6,
        out_specs=(vm, vm),
        scratch_shapes=[
            pltpu.VMEM((1, D), F32),
            pltpu.VMEM((ROWS, KVC), BF),
            pltpu.VMEM((ROWS, KVC), F32),
            pltpu.VMEM((TOK, 2560), BF),
            pltpu.VMEM((TOK, 2560), BF),
            pltpu.VMEM((TOK, D), BF),
            pltpu.VMEM((D, TOK), BF),
            pltpu.VMEM((8, 2, 4, 4, ROWS, 128), BF),
            pltpu.VMEM((TOK, 256), F32),
            pltpu.VMEM((TOK, KVC), BF),
            pltpu.VMEM((4, TOK, 256), BF),
            pltpu.VMEM((256, 1280), BF),
            pltpu.VMEM((256, 1280), BF),
            pltpu.VMEM((8, 2, 4, 4, ROWS, 128), BF),
            pltpu.VMEM((8, 4, 2, ROWS, 128), BF),
            pltpu.VMEM((8, 8, 2, ROWS, 128), BF),
            pltpu.VMEM((8, 2, 2, ROWS, 128), BF),
            pltpu.VMEM((8, 3, ROWS, 128), BF),
            pltpu.VMEM((4, 8, ROWS, 128), BF),
            pltpu.VMEM((4, ROWS, 128), BF),
            pltpu.VMEM((ROWS, 128), F32),
            pltpu.SemaphoreType.DMA((8, 17)),
            pltpu.SemaphoreType.DMA((8, 17)),
            pltpu.SemaphoreType.DMA((8, 17)),
            pltpu.SemaphoreType.DMA((8, 17)),
            pltpu.SemaphoreType.DMA((9, 3)),
            pltpu.SemaphoreType.DMA((9, 3)),
            pltpu.SemaphoreType.DMA((8,)),
            pltpu.SemaphoreType.DMA((8,)),
            pltpu.SemaphoreType.DMA((5,)),
        ],
        compiler_params=pltpu.CompilerParams(
            collective_id=0, has_side_effects=True, vmem_limit_bytes=60000000
        ),
    )(*arrays)


def local(hidden, norm_gain, queries, out_grad, kv_inner, kv_outer, momentum):
    fresh, average = step(
        hidden[0].reshape(TOK, D),
        norm_gain.reshape(1, D),
        kv_inner[0],
        queries[0].reshape(TOK, -1),
        out_grad[0].reshape(TOK, -1),
        kv_outer,
    )
    moment_new = momentum_decay * momentum + average
    outer_new = kv_outer - outer_rate * (momentum_decay * moment_new + average)
    blended = (blend_share * fresh + (1.0 - blend_share) * outer_new).astype(BF)
    return (blended[None], outer_new, moment_new)


def solution(mesh):
    split = Mesh(
        mesh.devices.reshape(2, 2, 2, 4, 4), GROUP + FSDP
    )
    return jax.shard_map(
        local,
        mesh=split,
        in_specs=(
            P(GROUP, FSDP, None, None),
            P(),
            P(GROUP, FSDP, None, None),
            P(GROUP, FSDP, None, None),
            P(GROUP, FSDP, None),
            P(FSDP, None),
            P(FSDP, None),
        ),
        out_specs=(P(GROUP, FSDP, None), P(FSDP, None), P(FSDP, None)),
        check_vma=False,
    )
```
